128 devices in a mesh: heads: 2 (over core), seq: 64 (over x, z, y).
Axes of the slice: x: 4, y: 4, z: 4, core: 2. Of those that a mesh axis runs over, the one named last changes fastest.
Arguments:
- tokens: bfloat16 [24576, 3072], P('seq', 'heads'), may hold values from -6 to 6
- w_query: bfloat16 [3072, 1536], P(None, 'heads'), may hold values from -1 to 1
- w_key: bfloat16 [3072, 1536], P(None, 'heads'), may hold values from -1 to 1
- w_value: bfloat16 [3072, 1536], P(None, 'heads'), may hold values from -0.109375 to 0.109375
- query_gain: float32 [128], replicated, may hold values from 0.5 to 8
- key_gain: float32 [128], replicated, may hold values from 0.5 to 8
- w_out: bfloat16 [1536, 3072], P('heads'), may hold values from -1.5 to 1.5
- key_tiles: int32 [64, 27], P('seq'), may hold values from 0 to 63, as said below
- key_counts: int32 [64], P('seq'), may hold values from 2 to 27, as said below
Outputs:
- mixed: bfloat16 [24576, 3072], P('seq', 'heads')
The draws below stay inside these ranges and needn't reach their ends.
Inputs may be any that keep to these rules, and one draw needn't show every extreme that they name: `key_tiles`: every used id is a tile whose grid place differs from tile g's by at most one in each of the three grid coordinates; slot 0 is g itself; used ids of one list are distinct; unused slots hold g. `key_counts`: some tile in every draw uses all 27 slots, and some tile uses exactly 2.
All inputs are finite; a program needn't handle non-finite values.
Results may differ from the reference program's by a relative error of at most 0.0095.
The reference program's roundings to bfloat16 on the way (of `query`, `key`, `value`, `weight` and `attended`) count: a program that leaves them out, or rounds other values in their place, can miss the bound.
Values may be sent and summed in bfloat16 or wider, within the bound.
A program may use at most 256 MiB of HBM per device.

```python
import jax
import jax.numpy as jnp
from jax import lax

D = 3072
HD = 128
HEADS = 12
TILE = 384
GRID_H = 4
GRID_W = 4
GRID_F = 4
NTILES = 64
TOKENS = 24576
KMAX = 27


def tile_lists(key):
    ntiles = GRID_F * GRID_H * GRID_W
    plane = GRID_H * GRID_W
    tiles = jnp.arange(ntiles, dtype=jnp.int32)
    tile_f = tiles // plane
    tile_h = tiles // GRID_W % GRID_H
    tile_w = tiles % GRID_W
    codes = jnp.array([c for c in range(27) if c != 13], dtype=jnp.int32)
    step_f = codes // 9 - 1
    step_h = codes // 3 % 3 - 1
    step_w = codes % 3 - 1
    new_f = tile_f[:, None] + step_f[None, :]
    new_h = tile_h[:, None] + step_h[None, :]
    new_w = tile_w[:, None] + step_w[None, :]
    valid = (new_f >= 0) & (new_f < GRID_F) & (new_h >= 0) & (new_h < GRID_H) & (new_w >= 0) & (new_w < GRID_W)
    other = tiles[:, None] + step_f[None, :] * plane + step_h[None, :] * GRID_W + step_w[None, :]
    row_keys = jax.random.split(jax.random.fold_in(key, 11), ntiles)
    ranks = jax.vmap(lambda k: jax.random.permutation(k, 26))(row_keys).astype(jnp.int32)
    order = jnp.argsort(jnp.where(valid, ranks, ranks + 100), axis=1)
    chosen = jnp.take_along_axis(other, order, axis=1)[:, :KMAX - 1]
    avail = jnp.sum(valid.astype(jnp.int32), axis=1)
    raw = jax.random.randint(jax.random.fold_in(key, 12), (ntiles,), 0, 1 << 20).astype(jnp.int32)
    drop = raw % ((avail + 1) // 2 + 1)
    counts = jnp.maximum(avail + 1 - drop, 2)
    counts = jnp.minimum(counts, KMAX)
    ties = jax.random.permutation(jax.random.fold_in(key, 13), ntiles).astype(jnp.int32)
    forced = jnp.argmax(jnp.where(avail + 1 >= KMAX, ties + ntiles, ties))
    fewest = jnp.min(avail)
    lowest = jnp.argmax(jnp.where(avail == fewest, ties + ntiles, ties))
    counts = jnp.where(tiles == forced, KMAX, counts)
    counts = jnp.where(tiles == lowest, 2, counts).astype(jnp.int32)
    slots = jnp.arange(KMAX, dtype=jnp.int32)
    whole = jnp.concatenate([tiles[:, None], chosen], axis=1)
    lists = jnp.where(slots[None, :] < counts[:, None], whole, tiles[:, None])
    return (lists.astype(jnp.int32), counts)


def draw_key_tiles(key, part):
    return tile_lists(key)[0]


def draw_key_counts(key, part):
    return tile_lists(key)[1]


def gain_values(key):
    return jax.random.uniform(key, (HD,), jnp.float32, 0.6, 1.6)


def draw_query_gain(key, part):
    return gain_values(jax.random.fold_in(key, 21))


def draw_key_gain(key, part):
    return gain_values(jax.random.fold_in(key, 22))


def projections(key):
    width = HEADS * HD
    factor = 1.0 / D ** 0.5
    base_q = jax.random.truncated_normal(jax.random.fold_in(key, 31), -6.0, 6.0, (D, width), jnp.float32) * factor
    base_k = jax.random.truncated_normal(jax.random.fold_in(key, 32), -6.0, 6.0, (D, width), jnp.float32) * factor
    return (jnp.clip(base_q, -1.0, 1.0), jnp.clip(base_k, -1.0, 1.0))


def draw_w_query(key, part):
    return projections(key)[0].astype(jnp.bfloat16)


def draw_w_key(key, part):
    return projections(key)[1].astype(jnp.bfloat16)


def draw_tokens(key, part):
    base = jax.random.truncated_normal(jax.random.fold_in(key, 41), -6.0, 6.0, (TOKENS, D), jnp.float32)
    return base.astype(jnp.bfloat16)


def shard_levels(stream_key, shape, shards, low, high):
    level, own = 1.0, jax.random.fold_in(stream_key, 6)
    for position, shards_of in shards:
        steps = jnp.exp(jax.random.uniform(jax.random.fold_in(own, position), (shards_of,), jnp.float32, low / len(shards), high / len(shards)))
        level = level * jnp.repeat(steps, shape[position] // shards_of).reshape([-1 if axis == position else 1 for axis in range(len(shape))])
    return level


def normal_values(key, extent, scale, reach, shards=(), kind=jnp.bfloat16):
    level = shard_levels(key, extent, shards, -0.22, 0.18) if shards else 1.0
    drawn = jax.random.normal(key, extent, jnp.float32) * scale * level
    return jnp.minimum(jnp.maximum(drawn, -reach), reach).astype(kind)


def setup_inputs(seed: int = 0) -> dict:
    keys = jax.random.split(jax.random.key(seed), 10)
    tokens = draw_tokens(jax.random.fold_in(keys[9], 71), 0)
    w_query = draw_w_query(jax.random.fold_in(keys[9], 71), 0)
    w_key = draw_w_key(jax.random.fold_in(keys[9], 71), 0)
    w_value = normal_values(keys[3], (D, HEADS * HD), D ** -0.5, 0.109375, ((1, 2),))
    query_gain = draw_query_gain(jax.random.fold_in(keys[9], 71), 0)
    key_gain = draw_key_gain(jax.random.fold_in(keys[9], 71), 0)
    w_out = normal_values(keys[6], (HEADS * HD, D), (HD // 8) ** -0.5, 1.5, ((0, 2),))
    key_tiles = draw_key_tiles(jax.random.fold_in(keys[9], 71), 0)
    key_counts = draw_key_counts(jax.random.fold_in(keys[9], 71), 0)
    return dict(tokens=tokens, w_query=w_query, w_key=w_key, w_value=w_value, query_gain=query_gain, key_gain=key_gain, w_out=w_out, key_tiles=key_tiles, key_counts=key_counts)


def normalize(proj, gain, heads):
    rows = proj.reshape(proj.shape[0], heads, -1)
    meansq = lax.optimization_barrier(jnp.mean(rows * rows, axis=-1, keepdims=True))
    return (rows * lax.rsqrt(meansq + 1e-06) * gain).astype(jnp.bfloat16).reshape(proj.shape[0], -1)

def reference(tokens, w_query, w_key, w_value, query_gain, key_gain, w_out, key_tiles, key_counts):
    query = normalize(jnp.dot(tokens, w_query, preferred_element_type=jnp.float32), query_gain, HEADS)
    key = normalize(jnp.dot(tokens, w_key, preferred_element_type=jnp.float32), key_gain, HEADS)
    value = jnp.dot(tokens, w_value, preferred_element_type=jnp.float32).astype(jnp.bfloat16)
    key_blocks = key.reshape(NTILES, TILE, HEADS, HD)
    value_blocks = value.reshape(NTILES, TILE, HEADS, HD)
    query_blocks = query.reshape(NTILES, TILE, HEADS, HD)
    scale = 1.0 / HD ** 0.5

    def one_tile(inputs):
        block, ids, count = inputs
        chosen_k = key_blocks[ids.astype(jnp.int32)].reshape(KMAX * TILE, HEADS, HD)
        chosen_v = value_blocks[ids.astype(jnp.int32)].reshape(KMAX * TILE, HEADS, HD)
        score = jnp.einsum('thd,khd->htk', block.astype(jnp.float32), chosen_k.astype(jnp.float32)) * scale
        valid = jnp.arange(KMAX * TILE, dtype=jnp.int32) // TILE < count
        score = jnp.where(valid[None, None, :], score, -jnp.inf)
        top = lax.optimization_barrier(jnp.max(score, axis=-1, keepdims=True))
        expo = jnp.exp(score - top)
        total = lax.optimization_barrier(jnp.sum(expo, axis=-1))
        weight = lax.optimization_barrier(expo.astype(jnp.bfloat16))
        summed = jnp.einsum('htk,khd->thd', weight.astype(jnp.float32), chosen_v.astype(jnp.float32))
        return (summed / jnp.transpose(total)[:, :, None]).astype(jnp.bfloat16)
    attended = lax.map(one_tile, (query_blocks, key_tiles, key_counts))
    attended = attended.reshape(TOKENS, HEADS * HD)
    return jnp.dot(attended, w_out, preferred_element_type=jnp.float32).astype(jnp.bfloat16)
```

```python
import functools
import math

import jax
import jax.numpy as jnp
from jax import lax
from jax.experimental import pallas as pl
from jax.experimental.pallas import tpu as pltpu
from jax.sharding import PartitionSpec as P

MESH = pl.DeviceIdType.MESH
GRID = 4
NEG = -1e30
FLOOR = -1e20
CENTRE = 21
TABLE = 48
BF16 = jnp.bfloat16
F32 = jnp.float32
NT = (((1,), (1,)), ((), ()))


def stride_of(axis):
    return 16 + (9 * axis * axis - 33 * axis) // 2


def neighbour(me, axis, by):
    stride = stride_of(axis)
    place = (me // stride) % GRID
    return me + ((place + by + GRID) % GRID - place) * stride


def kernel(
    blocks,
    x_hbm, wq_hbm, wk_hbm, wv_hbm, wo_hbm, qg_ref, kg_ref, ids_ref, cnt_ref,
    out_ref,
    xbuf, wbuf, wobuf, kbuf, vbuf, qbuf, acc, top, tot, osend, orecv, ssend, srecv, attbuf, table,
    load_sem, pair_send, pair_recv, tab_send, tab_recv,
    own_send, fwd_send, kv_recv, q_send, q_recv, o_send, o_recv,
):
    me = lax.axis_index("seq")
    half = lax.axis_index("heads")
    tile = x_hbm.shape[0]
    cols = x_hbm.shape[1]
    hd = qg_ref.shape[1]
    group = wq_hbm.shape[1] // hd
    hg = group // 2
    scale = math.log2(math.e) / math.sqrt(hd)

    def remote(src, dst, send, recv, device):
        return pltpu.make_async_remote_copy(
            src_ref=src, dst_ref=dst, send_sem=send, recv_sem=recv, device_id=device, device_id_type=MESH
        )

    loads = [pltpu.make_async_copy(x_hbm, xbuf.at[half], load_sem.at[0])]
    for pair in range(hg):
        for kind, ref in enumerate((wk_hbm, wv_hbm, wq_hbm)):
            loads.append(
                pltpu.make_async_copy(
                    ref.at[:, 2 * hd * pair : 2 * hd * (pair + 1)],
                    wbuf.at[kind, pair],
                    load_sem.at[1 + 3 * pair + kind],
                )
            )
    wo_own = pltpu.make_async_copy(
        wo_hbm.at[:, pl.ds(pl.multiple_of(half * cols, cols), cols)], wobuf.at[half], load_sem.at[1 + 3 * hg]
    )
    for copy in loads:
        copy.start()

    partner = (1 - half, me)
    barrier = pltpu.get_barrier_semaphore()
    for axis in range(3):
        for by in (1, -1):
            pl.semaphore_signal(barrier, inc=1, device_id=(half, neighbour(me, axis, by)), device_id_type=MESH)
    pl.semaphore_signal(barrier, inc=1, device_id=partner, device_id_type=MESH)
    pl.semaphore_wait(barrier, 7)

    x_copy = remote(x_hbm, xbuf.at[half], pair_send.at[0], pair_recv.at[0], partner)
    x_copy.start()
    wo_copy = remote(
        wo_hbm.at[:, pl.ds(pl.multiple_of((1 - half) * cols, cols), cols)],
        wobuf.at[half], pair_send.at[1], pair_recv.at[1], partner,
    )

    ids = ids_ref[...]
    used = lax.broadcasted_iota(jnp.int32, ids.shape, 1) < cnt_ref[...]
    wanted = lax.broadcasted_iota(jnp.int32, (TABLE, 1), 0) + (me - CENTRE)
    hit = jnp.where((ids == wanted) & used, 0.0, NEG)
    table[0] = jnp.broadcast_to(jnp.max(hit, axis=1, keepdims=True), (TABLE, hd))
    tab_copies = []
    for axis in range(3):
        for e, by in enumerate((1, -1)):
            tab_copies.append(
                remote(
                    table.at[0], table.at[2 + 2 * axis - e], tab_send.at[2 * axis + e],
                    tab_recv.at[2 * axis + 1 - e], (half, neighbour(me, axis, by)),
                )
            )
    for copy in tab_copies:
        copy.start()

    def kv_dst(h, grp, e):
        return kbuf.at[h, grp, pl.ds(e * tile, tile)], vbuf.at[h, grp, :, e * tile : (e + 1) * tile]

    def own_copies(h):
        o = h % 3
        out = []
        for role, grp in ((1, 1), (2, 2)):
            for e, by in enumerate((1, -1)):
                device = (half, neighbour(me, (o + role) % 3, by))
                for kv in range(2):
                    out.append(
                        remote(
                            kv_dst(h, 0, 0)[kv], kv_dst(h, grp, 1 - e)[kv], own_send.at[h, 2 * grp - 2 + e, kv],
                            kv_recv.at[h, grp, 1 - e, kv], device,
                        )
                    )
        return out

    def fwd_copies(h):
        o = h % 3
        out = []
        for b in range(2):
            for e, by in enumerate((1, -1)):
                device = (half, neighbour(me, (o + 2) % 3, by))
                for kv in range(2):
                    out.append(
                        remote(
                            kv_dst(h, 1, b)[kv], kv_dst(h, 3 + b, 1 - e)[kv], fwd_send.at[h, 2 * b + e, kv],
                            kv_recv.at[h, 3 + b, 1 - e, kv], device,
                        )
                    )
        return out

    def q_copies(h):
        return [
            remote(
                qbuf.at[h, 0:tile], qbuf.at[h, (2 - e) * tile : (3 - e) * tile], q_send.at[h, e],
                q_recv.at[h, 1 - e], (half, neighbour(me, h % 3, by)),
            )
            for e, by in enumerate((1, -1))
        ]

    def o_copies(h):
        out = []
        for e, by in enumerate((1, -1)):
            device = (half, neighbour(me, h % 3, by))
            out.append(remote(osend.at[h, e], orecv.at[h, 1 - e], o_send.at[h, e, 0], o_recv.at[h, 1 - e, 0], device))
            out.append(remote(ssend.at[h, e], srecv.at[h, 1 - e], o_send.at[h, e, 1], o_recv.at[h, 1 - e, 1], device))
        return out

    def start(copies):
        for copy in copies:
            copy.start()

    loads[0].wait()
    x_copy.wait_recv()

    def project(kind, pair):
        total = jnp.dot(xbuf[0], wbuf[kind, pair, :cols], preferred_element_type=F32)
        return total + jnp.dot(xbuf[1], wbuf[kind, pair, cols:], preferred_element_type=F32)

    def normal(rows, gain):
        meansq = jnp.mean(rows * rows, axis=-1, keepdims=True)
        return (rows * lax.rsqrt(meansq + 1e-06) * gain).astype(BF16)

    def one_pair(pair, carry):
        for kind, ref in enumerate((wk_hbm, wv_hbm)):
            pltpu.make_async_copy(
                ref.at[:, 0 : 2 * hd], wbuf.at[kind, pair], load_sem.at[1 + 3 * pair + kind]
            ).wait()
        proj = project(0, pair)
        for e in range(2):
            kbuf[2 * pair + e, 0, 0:tile, :] = normal(proj[:, e * hd : (e + 1) * hd], kg_ref[...])
        proj = project(1, pair)
        for e in range(2):
            vbuf[2 * pair + e, 0, :, 0:tile] = jnp.transpose(proj[:, e * hd : (e + 1) * hd]).astype(BF16)
        for e in range(2):
            start(own_copies(2 * pair + e))
        pltpu.make_async_copy(wq_hbm.at[:, 0 : 2 * hd], wbuf.at[2, pair], load_sem.at[3 + 3 * pair]).wait()
        proj = project(2, pair)
        for e in range(2):
            qbuf[2 * pair + e, 0:tile, :] = normal(proj[:, e * hd : (e + 1) * hd], qg_ref[...])
        for e in range(2):
            start(q_copies(2 * pair + e))
        return carry

    lax.fori_loop(0, hg, one_pair, 0)
    wo_own.start()
    wo_copy.start()
    for copy in tab_copies:
        copy.wait_recv()

    def shifts(h, b, g):
        o = h % 3
        sa, sb, sg = stride_of(o), stride_of((o + 1) % 3), stride_of((o + 2) % 3)
        parts = []
        for which, a in ((0, 0), (1, 1), (2, -1)):
            row = CENTRE - a * sa + b * sb + g * sg
            slot = 0 if which == 0 else 2 * o + which
            parts += [table[slot, pl.ds(row, 1), :]] * (tile // hd)
        return jnp.concatenate(parts, axis=1)

    def attend(h, grp, size, bias, first):
        keys = len(bias) * size
        wide = [slice(c, c + w) for c, w in blocks]

        def scores(cl):
            return lax.dot_general(kbuf[h, grp, 0:keys, :], qbuf[h, cl, :], NT, preferred_element_type=F32)

        def weigh(s, cl):
            parts = [s[t * size : (t + 1) * size] for t in range(len(bias))]
            new = jnp.full((1, s.shape[1]), FLOOR, F32) if first else top[h, 0:1, cl]
            old = new
            for part, shift in zip(parts, bias):
                new = jnp.maximum(new, jnp.max(part, axis=0, keepdims=True) + shift[:, cl])
            expo = [jnp.exp2(part * scale - (new - shift[:, cl]) * scale) for part, shift in zip(parts, bias)]
            sums = sum(jnp.sum(part, axis=0, keepdims=True) for part in expo)
            keep = None
            if not first:
                keep = jnp.exp2((old - new) * scale)
                sums = sums + tot[h, 0:1, cl] * keep
            tot[h, 0:1, cl] = sums
            top[h, 0:1, cl] = new
            return keep, jnp.concatenate([part.astype(BF16) for part in expo], axis=0)

        def add(keep, weight, cl):
            new = jnp.dot(vbuf[h, grp, :, 0:keys], weight, preferred_element_type=F32)
            acc[h, :, cl] = new if first else acc[h, :, cl] * keep + new

        s = scores(wide[0])
        for n, cl in enumerate(wide):
            later = scores(wide[n + 1]) if n + 1 < len(wide) else None
            keep, weight = weigh(s, cl)
            add(keep, weight, cl)
            s = later

    def own_step(h, carry):
        for copy in q_copies(h):
            copy.wait_recv()
        attend(h, 0, tile, [shifts(h, 0, 0)], True)
        return carry

    lax.fori_loop(0, group, own_step, 0)

    def step(t, carry):
        block, rest = t // 3, t % 3
        h = 3 * ((block // 2) % 2) + rest
        grp = 1 + block % 2 + 2 * (block // 4)
        for e in range(2):
            for kv in range(2):
                dst = kv_dst(h, grp, e)[kv]
                remote(dst, dst, own_send.at[h, 0, kv], kv_recv.at[h, grp, e, kv], partner).wait_recv()

        @pl.when(grp == 1)
        def _():
            start(fwd_copies(h))

        late = block // 4
        odd = block % 2
        b0 = late * (1 - 2 * odd) + (1 - late) * (1 - odd)
        b1 = late * (1 - 2 * odd) - (1 - late) * (1 - odd)
        g0 = late + (1 - late) * odd
        attend(h, grp, tile, [shifts(h, b0, g0), shifts(h, b1, 0 - g0)], False)

        @pl.when(grp == 4)
        def _():
            for e in range(2):
                cl = slice((1 + e) * tile, (2 + e) * tile)
                osend[h, e] = acc[h, :, cl].astype(BF16)
                ssend[h, e, 0:1, :] = top[h, 0:1, cl]
                ssend[h, e, 1:2, :] = tot[h, 0:1, cl]
            start(o_copies(h))

        return carry

    lax.fori_loop(0, 24, step, 0)

    def combine(h, carry):
        for copy in o_copies(h):
            copy.wait_recv()
        tops = [top[h, 0:1, 0:tile], srecv[h, 0, 0:1, :], srecv[h, 1, 0:1, :]]
        tots = [tot[h, 0:1, 0:tile], srecv[h, 0, 1:2, :], srecv[h, 1, 1:2, :]]
        high = jnp.maximum(tops[0], jnp.maximum(tops[1], tops[2]))
        share = [jnp.exp2((each - high) * scale) for each in tops]
        total = share[0] * tots[0] + share[1] * tots[1] + share[2] * tots[2]
        summed = acc[h, :, 0:tile] * share[0]
        for e in range(2):
            summed = summed + orecv[h, e].astype(F32) * share[1 + e]
        att = jnp.transpose(summed / total).astype(BF16)
        attbuf[half, :, pl.ds(pl.multiple_of(h * hd, hd), hd)] = att
        return carry

    lax.fori_loop(0, group, combine, 0)
    att_copy = remote(attbuf.at[half], attbuf.at[half], pair_send.at[2], pair_recv.at[2], partner)
    att_copy.start()
    wo_own.wait()
    wo_copy.wait_recv()
    att_copy.wait_recv()

    width = 2 * hd

    def project_out(c, carry):
        span = pl.ds(pl.multiple_of(c * width, width), width)
        total = jnp.dot(attbuf[0], wobuf[0, :, span], preferred_element_type=F32)
        total = total + jnp.dot(attbuf[1], wobuf[1, :, span], preferred_element_type=F32)
        out_ref[:, span] = total.astype(BF16)
        return carry

    lax.fori_loop(0, cols // width, project_out, 0)

    x_copy.wait_send()
    wo_copy.wait_send()
    att_copy.wait_send()
    for copy in tab_copies:
        copy.wait_send()

    def drain(h, carry):
        for copy in own_copies(h) + fwd_copies(h) + q_copies(h) + o_copies(h):
            copy.wait_send()
        return carry

    lax.fori_loop(0, group, drain, 0)


def on_device(blocks, tokens, w_query, w_key, w_value, query_gain, key_gain, w_out, key_tiles, key_counts):
    tile, cols = tokens.shape
    hd = query_gain.shape[0]
    heads = w_query.shape[1]
    group = heads // hd
    hg = group // 2
    any_space = pl.BlockSpec(memory_space=pl.ANY)
    vmem = pl.BlockSpec(memory_space=pltpu.VMEM)
    dma = pltpu.SemaphoreType.DMA
    return pl.pallas_call(
        functools.partial(kernel, blocks),
        out_shape=jax.ShapeDtypeStruct((tile, cols), BF16),
        in_specs=[any_space] * 5 + [vmem] * 4,
        out_specs=vmem,
        scratch_shapes=[
            pltpu.VMEM((2, tile, cols), BF16),
            pltpu.VMEM((3, hg, 2 * cols, 2 * hd), BF16),
            pltpu.VMEM((2, heads, cols), BF16),
            pltpu.VMEM((group, 5, 2 * tile, hd), BF16),
            pltpu.VMEM((group, 5, hd, 2 * tile), BF16),
            pltpu.VMEM((group, 3 * tile, hd), BF16),
            pltpu.VMEM((group, hd, 3 * tile), F32),
            pltpu.VMEM((group, 8, 3 * tile), F32),
            pltpu.VMEM((group, 8, 3 * tile), F32),
            pltpu.VMEM((group, 2, hd, tile), BF16),
            pltpu.VMEM((group, 2, hd, tile), BF16),
            pltpu.VMEM((group, 2, 8, tile), F32),
            pltpu.VMEM((group, 2, 8, tile), F32),
            pltpu.VMEM((2, tile, heads), BF16),
            pltpu.VMEM((7, TABLE, hd), F32),
            dma((2 + 3 * hg,)),
            dma((3,)),
            dma((3,)),
            dma((6,)),
            dma((6,)),
            dma((group, 4, 2)),
            dma((group, 4, 2)),
            dma((group, 5, 2, 2)),
            dma((group, 2)),
            dma((group, 2)),
            dma((group, 2, 2)),
            dma((group, 2, 2)),
        ],
        compiler_params=pltpu.CompilerParams(collective_id=0, has_side_effects=True, vmem_limit_bytes=66 * 2**20 - 2**21),
        name="tile_attention",
    )(
        tokens, w_query, w_key, w_value, w_out,
        query_gain.reshape(1, hd), key_gain.reshape(1, hd), key_tiles, key_counts.reshape(1, 1),
    )


BLOCKS = tuple((c * 128, 128) for c in range(9))


def solution(mesh):
    return jax.shard_map(
        functools.partial(on_device, BLOCKS),
        mesh=mesh,
        in_specs=(
            P("seq", "heads"),
            P(None, "heads"),
            P(None, "heads"),
            P(None, "heads"),
            P(),
            P(),
            P("heads", None),
            P("seq", None),
            P("seq"),
        ),
        out_specs=P("seq", "heads"),
        check_vma=False,
    )
```

```python
import functools
import math

import jax
import jax.numpy as jnp
from jax import lax
from jax.experimental import pallas as pl
from jax.experimental.pallas import tpu as pltpu
from jax.sharding import PartitionSpec as P

MESH = pl.DeviceIdType.MESH
GRID = 4
NEG = -1e30
FLOOR = -1e20
CENTRE = 21
TABLE = 48
BF16 = jnp.bfloat16
F32 = jnp.float32
NT = (((1,), (1,)), ((), ()))


def stride_of(axis):
    return 16 + (9 * axis * axis - 33 * axis) // 2


def neighbour(me, axis, by):
    stride = stride_of(axis)
    place = (me // stride) % GRID
    return me + ((place + by + GRID) % GRID - place) * stride


def kernel(
    blocks,
    x_hbm, wq_hbm, wk_hbm, wv_hbm, wo_hbm, qg_ref, kg_ref, ids_ref, cnt_ref,
    out_ref,
    xbuf, wbuf, wobuf, kbuf, vbuf, qbuf, acc, top, tot, osend, orecv, ssend, srecv, attbuf, table, partial, outacc,
    load_sem, pair_send, pair_recv, tab_send, tab_recv,
    own_send, fwd_send, kv_recv, q_send, q_recv, o_send, o_recv,
):
    me = lax.axis_index("seq")
    half = lax.axis_index("heads")
    tile = x_hbm.shape[0]
    cols = x_hbm.shape[1]
    hd = qg_ref.shape[1]
    group = wq_hbm.shape[1] // hd
    hg = group // 2
    scale = math.log2(math.e) / math.sqrt(hd)

    def remote(src, dst, send, recv, device):
        return pltpu.make_async_remote_copy(
            src_ref=src, dst_ref=dst, send_sem=send, recv_sem=recv, device_id=device, device_id_type=MESH
        )

    loads = [pltpu.make_async_copy(x_hbm, xbuf.at[half], load_sem.at[0])]
    for pair in range(hg):
        for kind, ref in enumerate((wk_hbm, wv_hbm, wq_hbm)):
            loads.append(
                pltpu.make_async_copy(
                    ref.at[:, 2 * hd * pair : 2 * hd * (pair + 1)],
                    wbuf.at[kind, pair],
                    load_sem.at[1 + 3 * pair + kind],
                )
            )
    part = hg * hd

    def wo_slices(wave, side):
        src = wo_hbm.at[wave * part : (wave + 1) * part, pl.ds(pl.multiple_of(side * cols, cols), cols)]
        return src, wobuf.at[wave, pl.ds(pl.multiple_of(half * part, part), part)]

    wo_own = [pltpu.make_async_copy(*wo_slices(wave, half), load_sem.at[1 + 3 * hg + wave]) for wave in range(2)]
    for copy in loads:
        copy.start()

    partner = (1 - half, me)
    barrier = pltpu.get_barrier_semaphore()
    for axis in range(3):
        for by in (1, -1):
            pl.semaphore_signal(barrier, inc=1, device_id=(half, neighbour(me, axis, by)), device_id_type=MESH)
    pl.semaphore_signal(barrier, inc=1, device_id=partner, device_id_type=MESH)
    pl.semaphore_wait(barrier, 7)

    x_copy = remote(x_hbm, xbuf.at[half], pair_send.at[0], pair_recv.at[0], partner)
    x_copy.start()
    wo_copy = [
        remote(*wo_slices(wave, 1 - half), pair_send.at[1 + wave], pair_recv.at[1 + wave], partner) for wave in range(2)
    ]

    ids = ids_ref[...]
    used = lax.broadcasted_iota(jnp.int32, ids.shape, 1) < cnt_ref[...]
    wanted = lax.broadcasted_iota(jnp.int32, (TABLE, 1), 0) + (me - CENTRE)
    hit = jnp.where((ids == wanted) & used, 0.0, NEG)
    table[0] = jnp.broadcast_to(jnp.max(hit, axis=1, keepdims=True), (TABLE, hd))
    tab_copies = []
    for axis in range(3):
        for e, by in enumerate((1, -1)):
            tab_copies.append(
                remote(
                    table.at[0], table.at[2 + 2 * axis - e], tab_send.at[2 * axis + e],
                    tab_recv.at[2 * axis + 1 - e], (half, neighbour(me, axis, by)),
                )
            )
    for copy in tab_copies:
        copy.start()

    def kv_dst(h, grp, e):
        return kbuf.at[h, grp, pl.ds(e * tile, tile)], vbuf.at[h, grp, :, e * tile : (e + 1) * tile]

    def own_copies(h):
        o = h % 3
        out = []
        for role, grp in ((1, 1), (2, 2)):
            for e, by in enumerate((1, -1)):
                device = (half, neighbour(me, (o + role) % 3, by))
                for kv in range(2):
                    out.append(
                        remote(
                            kv_dst(h, 0, 0)[kv], kv_dst(h, grp, 1 - e)[kv], own_send.at[h, 2 * grp - 2 + e, kv],
                            kv_recv.at[h, grp, 1 - e, kv], device,
                        )
                    )
        return out

    def fwd_copies(h):
        o = h % 3
        out = []
        for b in range(2):
            for e, by in enumerate((1, -1)):
                device = (half, neighbour(me, (o + 2) % 3, by))
                for kv in range(2):
                    out.append(
                        remote(
                            kv_dst(h, 1, b)[kv], kv_dst(h, 3 + b, 1 - e)[kv], fwd_send.at[h, 2 * b + e, kv],
                            kv_recv.at[h, 3 + b, 1 - e, kv], device,
                        )
                    )
        return out

    def q_copies(h):
        return [
            remote(
                qbuf.at[h, 0:tile], qbuf.at[h, (2 - e) * tile : (3 - e) * tile], q_send.at[h, e],
                q_recv.at[h, 1 - e], (half, neighbour(me, h % 3, by)),
            )
            for e, by in enumerate((1, -1))
        ]

    def o_copies(h):
        out = []
        for e, by in enumerate((1, -1)):
            device = (half, neighbour(me, h % 3, by))
            out.append(remote(osend.at[h, e], orecv.at[h, 1 - e], o_send.at[h, e, 0], o_recv.at[h, 1 - e, 0], device))
            out.append(remote(ssend.at[h, e], srecv.at[h, 1 - e], o_send.at[h, e, 1], o_recv.at[h, 1 - e, 1], device))
        return out

    def start(copies):
        for copy in copies:
            copy.start()

    loads[0].wait()

    def own_half(pair, carry):
        for kind, ref in ((2, wq_hbm), (0, wk_hbm), (1, wv_hbm)):
            pltpu.make_async_copy(
                ref.at[:, 0 : 2 * hd], wbuf.at[kind, pair], load_sem.at[1 + 3 * pair + kind]
            ).wait()
        rows = pl.ds(pl.multiple_of(half * cols, cols), cols)
        for kind in (2, 0, 1):
            partial[kind, pair] = jnp.dot(xbuf[half], wbuf[kind, pair, rows], preferred_element_type=F32)
        return carry

    lax.fori_loop(0, hg, own_half, 0)
    x_copy.wait_recv()

    def project(kind, pair):
        rows = pl.ds(pl.multiple_of((1 - half) * cols, cols), cols)
        return partial[kind, pair] + jnp.dot(xbuf[1 - half], wbuf[kind, pair, rows], preferred_element_type=F32)

    def normal(rows, gain):
        meansq = jnp.mean(rows * rows, axis=-1, keepdims=True)
        return (rows * lax.rsqrt(meansq + 1e-06) * gain).astype(BF16)

    def one_pair(pair, carry):
        proj = project(2, pair)
        for e in range(2):
            qbuf[2 * pair + e, 0:tile, :] = normal(proj[:, e * hd : (e + 1) * hd], qg_ref[...])
        proj = project(0, pair)
        for e in range(2):
            kbuf[2 * pair + e, 0, 0:tile, :] = normal(proj[:, e * hd : (e + 1) * hd], kg_ref[...])
        proj = project(1, pair)
        for e in range(2):
            vbuf[2 * pair + e, 0, :, 0:tile] = jnp.transpose(proj[:, e * hd : (e + 1) * hd]).astype(BF16)
        for e in range(2):
            start(q_copies(2 * pair + e))
        for e in range(2):
            start(own_copies(2 * pair + e))
        return carry

    lax.fori_loop(0, hg, one_pair, 0)
    start(wo_own)
    start(wo_copy)
    for copy in tab_copies:
        copy.wait_recv()

    def shifts(h, b, g):
        o = h % 3
        sa, sb, sg = stride_of(o), stride_of((o + 1) % 3), stride_of((o + 2) % 3)
        parts = []
        for which, a in ((0, 0), (1, 1), (2, -1)):
            row = CENTRE - a * sa + b * sb + g * sg
            slot = 0 if which == 0 else 2 * o + which
            parts += [table[slot, pl.ds(row, 1), :]] * (tile // hd)
        return jnp.concatenate(parts, axis=1)

    def attend(h, grp, size, bias, first, slots=(0, 1, 2)):
        keys = len(bias) * size
        wide = [slice(c, c + w) for c, w in blocks if c // tile in slots]

        def scores(cl):
            return lax.dot_general(kbuf[h, grp, 0:keys, :], qbuf[h, cl, :], NT, preferred_element_type=F32)

        def weigh(s, cl):
            parts = [s[t * size : (t + 1) * size] for t in range(len(bias))]
            new = jnp.full((1, s.shape[1]), FLOOR, F32) if first else top[h, 0:1, cl]
            old = new
            for part, shift in zip(parts, bias):
                new = jnp.maximum(new, jnp.max(part, axis=0, keepdims=True) + shift[:, cl])
            expo = [jnp.exp2(part * scale - (new - shift[:, cl]) * scale) for part, shift in zip(parts, bias)]
            sums = sum(jnp.sum(part, axis=0, keepdims=True) for part in expo)
            keep = None
            if not first:
                keep = jnp.exp2((old - new) * scale)
                sums = sums + tot[h, 0:1, cl] * keep
            tot[h, 0:1, cl] = sums
            top[h, 0:1, cl] = new
            return keep, jnp.concatenate([part.astype(BF16) for part in expo], axis=0)

        def add(keep, weight, cl):
            new = jnp.dot(vbuf[h, grp, :, 0:keys], weight, preferred_element_type=F32)
            acc[h, :, cl] = new if first else acc[h, :, cl] * keep + new

        s = scores(wide[0])
        for n, cl in enumerate(wide):
            later = scores(wide[n + 1]) if n + 1 < len(wide) else None
            keep, weight = weigh(s, cl)
            add(keep, weight, cl)
            s = later

    def own_step(h, carry):
        for copy in q_copies(h):
            copy.wait_recv()
        attend(h, 0, tile, [shifts(h, 0, 0)], True)
        return carry

    lax.fori_loop(0, hg, own_step, 0)

    def place(t):
        block = t // 3
        return 3 * ((block // 2) % 2) + t % 3, 1 + block % 2 + 2 * (block // 4)

    def group_bias(h, t):
        block = t // 3
        late, odd = block // 4, block % 2
        b0 = late * (1 - 2 * odd) + (1 - late) * (1 - odd)
        b1 = late * (1 - 2 * odd) - (1 - late) * (1 - odd)
        g0 = late + (1 - late) * odd
        return [shifts(h, b0, g0), shifts(h, b1, 0 - g0)]

    def arrive(h, grp):
        for e in range(2):
            for kv in range(2):
                dst = kv_dst(h, grp, e)[kv]
                remote(dst, dst, own_send.at[h, 0, kv], kv_recv.at[h, grp, e, kv], partner).wait_recv()

    def give_back(h):
        for e in range(2):
            cl = slice((1 + e) * tile, (2 + e) * tile)
            osend[h, e] = acc[h, :, cl].astype(BF16)
            ssend[h, e, 0:1, :] = top[h, 0:1, cl]
            ssend[h, e, 1:2, :] = tot[h, 0:1, cl]
        start(o_copies(h))

    def step(t, carry):
        h, grp = place(t)

        @pl.when(t // 3 == 2)
        def _():
            own_step(h, 0)

        arrive(h, grp)

        @pl.when(grp == 1)
        def _():
            start(fwd_copies(h))

        attend(h, grp, tile, group_bias(h, t), False)

        @pl.when(grp == 4)
        def _():
            give_back(h)

        return carry

    def last_others(t, carry):
        h, grp = place(t)
        arrive(h, grp)
        attend(h, grp, tile, group_bias(h, t), False, (1, 2))
        give_back(h)
        return carry

    def last_own(t, carry):
        h, grp = place(t)
        attend(h, grp, tile, group_bias(h, t), False, (0,))
        return carry

    def combine(h, carry):
        for copy in o_copies(h):
            copy.wait_recv()
        tops = [top[h, 0:1, 0:tile], srecv[h, 0, 0:1, :], srecv[h, 1, 0:1, :]]
        tots = [tot[h, 0:1, 0:tile], srecv[h, 0, 1:2, :], srecv[h, 1, 1:2, :]]
        high = jnp.maximum(tops[0], jnp.maximum(tops[1], tops[2]))
        share = [jnp.exp2((each - high) * scale) for each in tops]
        total = share[0] * tots[0] + share[1] * tots[1] + share[2] * tots[2]
        summed = acc[h, :, 0:tile] * share[0]
        for e in range(2):
            summed = summed + orecv[h, e].astype(F32) * share[1 + e]
        att = jnp.transpose(summed / total).astype(BF16)
        attbuf[h // 3, half, :, pl.ds(pl.multiple_of((h % 3) * hd, hd), hd)] = att
        return carry

    width = 2 * hd
    att_copies = [
        remote(attbuf.at[wave, half], attbuf.at[wave, half], pair_send.at[3 + wave], pair_recv.at[3 + wave], partner)
        for wave in range(2)
    ]

    def project_out(wave, c):
        span = pl.ds(pl.multiple_of(c * width, width), width)
        total = jnp.dot(attbuf[wave, 0], wobuf[wave, 0:part, span], preferred_element_type=F32)
        return span, total + jnp.dot(attbuf[wave, 1], wobuf[wave, part:, span], preferred_element_type=F32)

    def out_first(c, carry):
        span, total = project_out(0, c)
        outacc[:, span] = total
        return carry

    def out_second(c, carry):
        span, total = project_out(1, c)
        out_ref[:, span] = (outacc[:, span] + total).astype(BF16)
        return carry

    lax.fori_loop(0, 21, step, 0)
    lax.fori_loop(21, 24, last_others, 0)
    lax.fori_loop(0, hg, combine, 0)
    att_copies[0].start()
    lax.fori_loop(21, 24, last_own, 0)
    for copy in wo_own:
        copy.wait()
    for copy in wo_copy:
        copy.wait_recv()
    att_copies[0].wait_recv()
    lax.fori_loop(0, cols // width, out_first, 0)
    lax.fori_loop(hg, group, combine, 0)
    att_copies[1].start()
    att_copies[1].wait_recv()
    lax.fori_loop(0, cols // width, out_second, 0)

    x_copy.wait_send()
    for copy in wo_copy + att_copies + tab_copies:
        copy.wait_send()

    def drain(h, carry):
        for copy in own_copies(h) + fwd_copies(h) + q_copies(h) + o_copies(h):
            copy.wait_send()
        return carry

    lax.fori_loop(0, group, drain, 0)


def on_device(blocks, tokens, w_query, w_key, w_value, query_gain, key_gain, w_out, key_tiles, key_counts):
    tile, cols = tokens.shape
    hd = query_gain.shape[0]
    heads = w_query.shape[1]
    group = heads // hd
    hg = group // 2
    any_space = pl.BlockSpec(memory_space=pl.ANY)
    vmem = pl.BlockSpec(memory_space=pltpu.VMEM)
    dma = pltpu.SemaphoreType.DMA
    return pl.pallas_call(
        functools.partial(kernel, blocks),
        out_shape=jax.ShapeDtypeStruct((tile, cols), BF16),
        in_specs=[any_space] * 5 + [vmem] * 4,
        out_specs=vmem,
        scratch_shapes=[
            pltpu.VMEM((2, tile, cols), BF16),
            pltpu.VMEM((3, hg, 2 * cols, 2 * hd), BF16),
            pltpu.VMEM((2, heads, cols), BF16),
            pltpu.VMEM((group, 5, 2 * tile, hd), BF16),
            pltpu.VMEM((group, 5, hd, 2 * tile), BF16),
            pltpu.VMEM((group, 3 * tile, hd), BF16),
            pltpu.VMEM((group, hd, 3 * tile), F32),
            pltpu.VMEM((group, 8, 3 * tile), F32),
            pltpu.VMEM((group, 8, 3 * tile), F32),
            pltpu.VMEM((group, 2, hd, tile), BF16),
            pltpu.VMEM((group, 2, hd, tile), BF16),
            pltpu.VMEM((group, 2, 8, tile), F32),
            pltpu.VMEM((group, 2, 8, tile), F32),
            pltpu.VMEM((2, 2, tile, hg * hd), BF16),
            pltpu.VMEM((7, TABLE, hd), F32),
            pltpu.VMEM((3, hg, tile, 2 * hd), F32),
            pltpu.VMEM((tile, cols), F32),
            dma((3 + 3 * hg,)),
            dma((5,)),
            dma((5,)),
            dma((6,)),
            dma((6,)),
            dma((group, 4, 2)),
            dma((group, 4, 2)),
            dma((group, 5, 2, 2)),
            dma((group, 2)),
            dma((group, 2)),
            dma((group, 2, 2)),
            dma((group, 2, 2)),
        ],
        compiler_params=pltpu.CompilerParams(collective_id=0, has_side_effects=True, vmem_limit_bytes=66 * 2**20 - 2**21),
        name="tile_attention",
    )(
        tokens, w_query, w_key, w_value, w_out,
        query_gain.reshape(1, hd), key_gain.reshape(1, hd), key_tiles, key_counts.reshape(1, 1),
    )


BLOCKS = tuple((c * 128, 128) for c in range(9))


def solution(mesh):
    return jax.shard_map(
        functools.partial(on_device, BLOCKS),
        mesh=mesh,
        in_specs=(
            P("seq", "heads"),
            P(None, "heads"),
            P(None, "heads"),
            P(None, "heads"),
            P(),
            P(),
            P("heads", None),
            P("seq", None),
            P("seq"),
        ),
        out_specs=P("seq", "heads"),
        check_vma=False,
    )
```

```python
import functools
import math

import jax
import jax.numpy as jnp
from jax import lax
from jax.experimental import pallas as pl
from jax.experimental.pallas import tpu as pltpu
from jax.sharding import PartitionSpec as P

MESH = pl.DeviceIdType.MESH
GRID = 4
NEG = -1e30
FLOOR = -1e20
CENTRE = 21
TABLE = 48
BF16 = jnp.bfloat16
F32 = jnp.float32
NT = (((1,), (1,)), ((), ()))


def stride_of(axis):
    return 16 + (9 * axis * axis - 33 * axis) // 2


def neighbour(me, axis, by):
    stride = stride_of(axis)
    place = (me // stride) % GRID
    return me + ((place + by + GRID) % GRID - place) * stride


def kernel(
    blocks,
    x_hbm, wq_hbm, wk_hbm, wv_hbm, wo_hbm, qg_ref, kg_ref, ids_ref, cnt_ref,
    out_ref,
    xbuf, wbuf, wobuf, kbuf, vbuf, qbuf, acc, top, tot, osend, orecv, ssend, srecv, attbuf, table, partial, outacc, pbuf,
    load_sem, pair_send, pair_recv, tab_send, tab_recv,
    own_send, fwd_send, kv_recv, q_send, q_recv, o_send, o_recv,
):
    me = lax.axis_index("seq")
    half = lax.axis_index("heads")
    tile = x_hbm.shape[0]
    cols = x_hbm.shape[1]
    hd = qg_ref.shape[1]
    group = wq_hbm.shape[1] // hd
    hg = group // 2
    scale = math.log2(math.e) / math.sqrt(hd)

    def remote(src, dst, send, recv, device):
        return pltpu.make_async_remote_copy(
            src_ref=src, dst_ref=dst, send_sem=send, recv_sem=recv, device_id=device, device_id_type=MESH
        )

    loads = [pltpu.make_async_copy(x_hbm, xbuf.at[half], load_sem.at[0])]
    for pair in range(hg):
        for kind, ref in enumerate((wk_hbm, wv_hbm, wq_hbm)):
            loads.append(
                pltpu.make_async_copy(
                    ref.at[:, 2 * hd * pair : 2 * hd * (pair + 1)],
                    wbuf.at[kind, pair],
                    load_sem.at[1 + 3 * pair + kind],
                )
            )
    part = hg * hd

    def wo_slices(wave, side):
        src = wo_hbm.at[wave * part : (wave + 1) * part, pl.ds(pl.multiple_of(side * cols, cols), cols)]
        return src, wobuf.at[wave, pl.ds(pl.multiple_of(half * part, part), part)]

    wo_own = [pltpu.make_async_copy(*wo_slices(wave, half), load_sem.at[1 + 3 * hg + wave]) for wave in range(2)]
    for copy in loads:
        copy.start()

    partner = (1 - half, me)
    barrier = pltpu.get_barrier_semaphore()
    for axis in range(3):
        for by in (1, -1):
            pl.semaphore_signal(barrier, inc=1, device_id=(half, neighbour(me, axis, by)), device_id_type=MESH)
    pl.semaphore_signal(barrier, inc=1, device_id=partner, device_id_type=MESH)
    pl.semaphore_wait(barrier, 7)

    x_copy = remote(x_hbm, xbuf.at[half], pair_send.at[0], pair_recv.at[0], partner)
    x_copy.start()
    wo_copy = [
        remote(*wo_slices(wave, 1 - half), pair_send.at[1 + wave], pair_recv.at[1 + wave], partner) for wave in range(2)
    ]

    ids = ids_ref[...]
    used = lax.broadcasted_iota(jnp.int32, ids.shape, 1) < cnt_ref[...]
    wanted = lax.broadcasted_iota(jnp.int32, (TABLE, 1), 0) + (me - CENTRE)
    hit = jnp.where((ids == wanted) & used, 0.0, NEG)
    table[0] = jnp.broadcast_to(jnp.max(hit, axis=1, keepdims=True), (TABLE, hd))
    tab_copies = []
    for axis in range(3):
        for e, by in enumerate((1, -1)):
            tab_copies.append(
                remote(
                    table.at[0], table.at[2 + 2 * axis - e], tab_send.at[2 * axis + e],
                    tab_recv.at[2 * axis + 1 - e], (half, neighbour(me, axis, by)),
                )
            )
    for copy in tab_copies:
        copy.start()

    def kv_dst(h, grp, e):
        return kbuf.at[h, grp, pl.ds(e * tile, tile)], vbuf.at[h, grp, :, e * tile : (e + 1) * tile]

    def own_copies(h, roles=(1, 2)):
        o = h % 3
        out = []
        for role in roles:
            grp = role
            for e, by in enumerate((1, -1)):
                device = (half, neighbour(me, (o + role) % 3, by))
                for kv in range(2):
                    out.append(
                        remote(
                            kv_dst(h, 0, 0)[kv], kv_dst(h, grp, 1 - e)[kv], own_send.at[h, 2 * grp - 2 + e, kv],
                            kv_recv.at[h, grp, 1 - e, kv], device,
                        )
                    )
        return out

    def fwd_copies(h):
        o = h % 3
        out = []
        for b in range(2):
            for e, by in enumerate((1, -1)):
                device = (half, neighbour(me, (o + 2) % 3, by))
                for kv in range(2):
                    out.append(
                        remote(
                            kv_dst(h, 1, b)[kv], kv_dst(h, 3 + b, 1 - e)[kv], fwd_send.at[h, 2 * b + e, kv],
                            kv_recv.at[h, 3 + b, 1 - e, kv], device,
                        )
                    )
        return out

    def q_copies(h):
        return [
            remote(
                qbuf.at[h, 0:tile], qbuf.at[h, (2 - e) * tile : (3 - e) * tile], q_send.at[h, e],
                q_recv.at[h, 1 - e], (half, neighbour(me, h % 3, by)),
            )
            for e, by in enumerate((1, -1))
        ]

    def o_copies(h):
        out = []
        for e, by in enumerate((1, -1)):
            device = (half, neighbour(me, h % 3, by))
            out.append(remote(osend.at[h, e], orecv.at[h, 1 - e], o_send.at[h, e, 0], o_recv.at[h, 1 - e, 0], device))
            out.append(remote(ssend.at[h, e], srecv.at[h, 1 - e], o_send.at[h, e, 1], o_recv.at[h, 1 - e, 1], device))
        return out

    def start(copies):
        for copy in copies:
            copy.start()

    loads[0].wait()

    def own_half(pair, carry):
        for kind, ref in ((2, wq_hbm), (0, wk_hbm), (1, wv_hbm)):
            pltpu.make_async_copy(
                ref.at[:, 0 : 2 * hd], wbuf.at[kind, pair], load_sem.at[1 + 3 * pair + kind]
            ).wait()
        rows = pl.ds(pl.multiple_of(half * cols, cols), cols)
        for kind in (2, 0, 1):
            partial[kind, pair] = jnp.dot(xbuf[half], wbuf[kind, pair, rows], preferred_element_type=F32)
        return carry

    lax.fori_loop(0, hg, own_half, 0)
    x_copy.wait_recv()

    def project(kind, pair):
        rows = pl.ds(pl.multiple_of((1 - half) * cols, cols), cols)
        return partial[kind, pair] + jnp.dot(xbuf[1 - half], wbuf[kind, pair, rows], preferred_element_type=F32)

    def normal(rows, gain):
        meansq = jnp.mean(rows * rows, axis=-1, keepdims=True)
        return (rows * lax.rsqrt(meansq + 1e-06) * gain).astype(BF16)

    def one_pair(pair, carry):
        proj = project(2, pair)
        for e in range(2):
            qbuf[2 * pair + e, 0:tile, :] = normal(proj[:, e * hd : (e + 1) * hd], qg_ref[...])
        proj = project(0, pair)
        for e in range(2):
            kbuf[2 * pair + e, 0, 0:tile, :] = normal(proj[:, e * hd : (e + 1) * hd], kg_ref[...])
        proj = project(1, pair)
        for e in range(2):
            vbuf[2 * pair + e, 0, :, 0:tile] = jnp.transpose(proj[:, e * hd : (e + 1) * hd]).astype(BF16)
        for e in range(2):

            @pl.when(2 * pair + e < hg)
            def _():
                start(q_copies(2 * pair + e) + own_copies(2 * pair + e, (1,)))

        return carry

    lax.fori_loop(0, hg, one_pair, 0)
    start(wo_own)
    start(wo_copy)
    for copy in tab_copies:
        copy.wait_recv()

    def shifts(h, b, g):
        o = h % 3
        sa, sb, sg = stride_of(o), stride_of((o + 1) % 3), stride_of((o + 2) % 3)
        parts = []
        for which, a in ((0, 0), (1, 1), (2, -1)):
            row = CENTRE - a * sa + b * sb + g * sg
            slot = 0 if which == 0 else 2 * o + which
            parts += [table[slot, pl.ds(row, 1), :]] * (tile // hd)
        return jnp.concatenate(parts, axis=1)

    def attend(h, work, slots=(0, 1, 2)):
        wide = [slice(c, c + w) for c, w in blocks if c // tile in slots]
        lots = [(*each, wide[n : n + 2]) for each in work for n in range(0, len(wide), 2)]
        items = [(grp, len(bias) * tile, cl) for grp, bias, first, lot in lots for cl in lot]

        def scores(grp, keys, cl):
            return lax.dot_general(kbuf[h, grp, 0:keys, :], qbuf[h, cl, :], NT, preferred_element_type=F32)

        def weigh(s, bias, first, cl, slot, span):
            parts = [s[t * tile : (t + 1) * tile] for t in range(len(bias))]
            new = jnp.full((1, s.shape[1]), FLOOR, F32) if first else top[h, 0:1, cl]
            old = new
            for part, shift in zip(parts, bias):
                new = jnp.maximum(new, jnp.max(part, axis=0, keepdims=True) + shift[:, cl])
            sums = None
            for t, (part, shift) in enumerate(zip(parts, bias)):
                expo = jnp.exp2(part * scale - (new - shift[:, cl]) * scale)
                pbuf[slot, t * tile : (t + 1) * tile, span] = expo.astype(BF16)
                fold = jnp.sum(expo, axis=0, keepdims=True)
                sums = fold if sums is None else sums + fold
            keep = None
            if not first:
                keep = jnp.exp2((old - new) * scale)
                sums = sums + tot[h, 0:1, cl] * keep
            tot[h, 0:1, cl] = sums
            top[h, 0:1, cl] = new
            return keep

        def add(slot, grp, keys, first, lot, keeps):
            cl = slice(lot[0].start, lot[-1].stop)
            new = jnp.dot(
                vbuf[h, grp, :, 0:keys], pbuf[slot, 0:keys, 0 : cl.stop - cl.start], preferred_element_type=F32
            )
            acc[h, :, cl] = new if first else acc[h, :, cl] * jnp.concatenate(keeps, axis=1) + new

        s = scores(*items[0])
        count = 0
        last = None
        for n, (grp, bias, first, lot) in enumerate(lots):
            keeps = []
            for cl in lot:
                count += 1
                later = scores(*items[count]) if count < len(items) else None
                offset = cl.start - lot[0].start
                keeps.append(weigh(s, bias, first, cl, n % 2, slice(offset, offset + cl.stop - cl.start)))
                s = later
            if last is not None:
                add(*last)
            last = (n % 2, grp, len(bias) * tile, first, lot, keeps)
        add(*last)

    def arrive(h, grp):
        for e in range(2):
            for kv in range(2):
                dst = kv_dst(h, grp, e)[kv]
                remote(dst, dst, own_send.at[h, 0, kv], kv_recv.at[h, grp, e, kv], partner).wait_recv()

    def own_step(h, carry):
        for copy in q_copies(h):
            copy.wait_recv()
        attend(h, [(0, [shifts(h, 0, 0)], True)])
        return carry

    def first_own(h, carry):
        start(own_copies(h, (2,)))
        return own_step(h, carry)

    def forward(h, carry):
        arrive(h, 1)
        start(fwd_copies(h))
        return carry

    def send_first(h, carry):
        start(q_copies(h) + own_copies(h, (1,)))
        return carry

    def send_second(h, carry):
        start(own_copies(h, (2,)))
        return carry

    def give_back(h):
        for e in range(2):
            cl = slice((1 + e) * tile, (2 + e) * tile)
            osend[h, e] = acc[h, :, cl].astype(BF16)
            ssend[h, e, 0:1, :] = top[h, 0:1, cl]
            ssend[h, e, 1:2, :] = tot[h, 0:1, cl]
        start(o_copies(h))

    def two_groups(h, late):
        first = [shifts(h, 1, late), shifts(h, 2 * late - 1, 0 - late)]
        second = [shifts(h, 0 - late, 1), shifts(h, 0 - late, -1)]
        return [(1 + 2 * late, first, False), (2 + 2 * late, second, False)]

    def step(t, carry):
        block, rest = t // 3, t % 3
        late = block % 2
        h = 3 * (block // 2) + rest

        @pl.when(t == 2)
        def _():
            lax.fori_loop(hg, group, send_first, 0)

        @pl.when(t == 3)
        def _():
            lax.fori_loop(hg, group, send_second, 0)

        @pl.when(t == 5)
        def _():
            lax.fori_loop(hg, group, forward, 0)

        @pl.when(block == 2)
        def _():
            own_step(h, 0)

        @pl.when(late == 0)
        def _():
            arrive(h, 2)

        @pl.when(late == 1)
        def _():
            arrive(h, 3)
            arrive(h, 4)

        attend(h, two_groups(h, late))

        @pl.when(late == 1)
        def _():
            give_back(h)

        return carry

    def last_others(h, carry):
        arrive(h, 3)
        arrive(h, 4)
        attend(h, two_groups(h, 1), (1, 2))
        give_back(h)
        return carry

    def last_own(h, carry):
        attend(h, two_groups(h, 1), (0,))
        return carry

    def combine(h, carry):
        for copy in o_copies(h):
            copy.wait_recv()
        tops = [top[h, 0:1, 0:tile], srecv[h, 0, 0:1, :], srecv[h, 1, 0:1, :]]
        tots = [tot[h, 0:1, 0:tile], srecv[h, 0, 1:2, :], srecv[h, 1, 1:2, :]]
        high = jnp.maximum(tops[0], jnp.maximum(tops[1], tops[2]))
        share = [jnp.exp2((each - high) * scale) for each in tops]
        total = share[0] * tots[0] + share[1] * tots[1] + share[2] * tots[2]
        summed = acc[h, :, 0:tile] * share[0]
        for e in range(2):
            summed = summed + orecv[h, e].astype(F32) * share[1 + e]
        att = jnp.transpose(summed / total).astype(BF16)
        attbuf[h // 3, half, :, pl.ds(pl.multiple_of((h % 3) * hd, hd), hd)] = att
        return carry

    width = 2 * hd
    att_copies = [
        remote(attbuf.at[wave, half], attbuf.at[wave, half], pair_send.at[3 + wave], pair_recv.at[3 + wave], partner)
        for wave in range(2)
    ]

    def project_out(wave, c):
        span = pl.ds(pl.multiple_of(c * width, width), width)
        total = jnp.dot(attbuf[wave, 0], wobuf[wave, 0:part, span], preferred_element_type=F32)
        return span, total + jnp.dot(attbuf[wave, 1], wobuf[wave, part:, span], preferred_element_type=F32)

    def out_first(c, carry):
        span, total = project_out(0, c)
        outacc[:, span] = total
        return carry

    def out_second(c, carry):
        span, total = project_out(1, c)
        out_ref[:, span] = (outacc[:, span] + total).astype(BF16)
        return carry

    lax.fori_loop(0, hg, first_own, 0)
    lax.fori_loop(0, hg, forward, 0)
    lax.fori_loop(0, 9, step, 0)
    lax.fori_loop(hg, group, last_others, 0)
    lax.fori_loop(0, hg, combine, 0)
    att_copies[0].start()
    lax.fori_loop(hg, group, last_own, 0)
    for copy in wo_own:
        copy.wait()
    for copy in wo_copy:
        copy.wait_recv()
    att_copies[0].wait_recv()
    lax.fori_loop(0, cols // width, out_first, 0)
    lax.fori_loop(hg, group, combine, 0)
    att_copies[1].start()
    att_copies[1].wait_recv()
    lax.fori_loop(0, cols // width, out_second, 0)

    x_copy.wait_send()
    for copy in wo_copy + att_copies + tab_copies:
        copy.wait_send()

    def drain(h, carry):
        for copy in own_copies(h) + fwd_copies(h) + q_copies(h) + o_copies(h):
            copy.wait_send()
        return carry

    lax.fori_loop(0, group, drain, 0)


def on_device(blocks, tokens, w_query, w_key, w_value, query_gain, key_gain, w_out, key_tiles, key_counts):
    tile, cols = tokens.shape
    hd = query_gain.shape[0]
    heads = w_query.shape[1]
    group = heads // hd
    hg = group // 2
    any_space = pl.BlockSpec(memory_space=pl.ANY)
    vmem = pl.BlockSpec(memory_space=pltpu.VMEM)
    dma = pltpu.SemaphoreType.DMA
    return pl.pallas_call(
        functools.partial(kernel, blocks),
        out_shape=jax.ShapeDtypeStruct((tile, cols), BF16),
        in_specs=[any_space] * 5 + [vmem] * 4,
        out_specs=vmem,
        scratch_shapes=[
            pltpu.VMEM((2, tile, cols), BF16),
            pltpu.VMEM((3, hg, 2 * cols, 2 * hd), BF16),
            pltpu.VMEM((2, heads, cols), BF16),
            pltpu.VMEM((group, 5, 2 * tile, hd), BF16),
            pltpu.VMEM((group, 5, hd, 2 * tile), BF16),
            pltpu.VMEM((group, 3 * tile, hd), BF16),
            pltpu.VMEM((group, hd, 3 * tile), F32),
            pltpu.VMEM((group, 8, 3 * tile), F32),
            pltpu.VMEM((group, 8, 3 * tile), F32),
            pltpu.VMEM((group, 2, hd, tile), BF16),
            pltpu.VMEM((group, 2, hd, tile), BF16),
            pltpu.VMEM((group, 2, 8, tile), F32),
            pltpu.VMEM((group, 2, 8, tile), F32),
            pltpu.VMEM((2, 2, tile, hg * hd), BF16),
            pltpu.VMEM((7, TABLE, hd), F32),
            pltpu.VMEM((3, hg, tile, 2 * hd), F32),
            pltpu.VMEM((tile, cols), F32),
            pltpu.VMEM((2, 2 * tile, 2 * hd), BF16),
            dma((3 + 3 * hg,)),
            dma((5,)),
            dma((5,)),
            dma((6,)),
            dma((6,)),
            dma((group, 4, 2)),
            dma((group, 4, 2)),
            dma((group, 5, 2, 2)),
            dma((group, 2)),
            dma((group, 2)),
            dma((group, 2, 2)),
            dma((group, 2, 2)),
        ],
        compiler_params=pltpu.CompilerParams(collective_id=0, has_side_effects=True, vmem_limit_bytes=66 * 2**20 - 2**21),
        name="tile_attention",
    )(
        tokens, w_query, w_key, w_value, w_out,
        query_gain.reshape(1, hd), key_gain.reshape(1, hd), key_tiles, key_counts.reshape(1, 1),
    )


BLOCKS = tuple((c * 128, 128) for c in range(9))


def solution(mesh):
    return jax.shard_map(
        functools.partial(on_device, BLOCKS),
        mesh=mesh,
        in_specs=(
            P("seq", "heads"),
            P(None, "heads"),
            P(None, "heads"),
            P(None, "heads"),
            P(),
            P(),
            P("heads", None),
            P("seq", None),
            P("seq"),
        ),
        out_specs=P("seq", "heads"),
        check_vma=False,
    )
```

```python
import functools
import math

import jax
import jax.numpy as jnp
from jax import lax
from jax.experimental import pallas as pl
from jax.experimental.pallas import tpu as pltpu
from jax.sharding import PartitionSpec as P

MESH = pl.DeviceIdType.MESH
GRID = 4
NEG = -1e30
FLOOR = -1e20
CENTRE = 21
TABLE = 48
BF16 = jnp.bfloat16
F32 = jnp.float32
NT = (((1,), (1,)), ((), ()))


def stride_of(axis):
    return 16 + (9 * axis * axis - 33 * axis) // 2


def neighbour(me, axis, by):
    stride = stride_of(axis)
    place = (me // stride) % GRID
    return me + ((place + by + GRID) % GRID - place) * stride


def kernel(
    blocks,
    x_hbm, wq_hbm, wk_hbm, wv_hbm, wo_hbm, qg_ref, kg_ref, ids_ref, cnt_ref,
    out_ref,
    xbuf, wbuf, wobuf, kbuf, vbuf, qbuf, acc, top, tot, osend, orecv, ssend, srecv, attbuf, table, partial, outacc,
    load_sem, pair_send, pair_recv, tab_send, tab_recv,
    own_send, fwd_send, kv_recv, q_send, q_recv, o_send, o_recv,
):
    me = lax.axis_index("seq")
    half = lax.axis_index("heads")
    tile = x_hbm.shape[0]
    cols = x_hbm.shape[1]
    hd = qg_ref.shape[1]
    group = wq_hbm.shape[1] // hd
    hg = group // 2
    scale = math.log2(math.e) / math.sqrt(hd)

    def remote(src, dst, send, recv, device):
        return pltpu.make_async_remote_copy(
            src_ref=src, dst_ref=dst, send_sem=send, recv_sem=recv, device_id=device, device_id_type=MESH
        )

    loads = [pltpu.make_async_copy(x_hbm, xbuf.at[half], load_sem.at[0])]
    for pair in range(hg):
        for kind, ref in enumerate((wk_hbm, wv_hbm, wq_hbm)):
            loads.append(
                pltpu.make_async_copy(
                    ref.at[:, 2 * hd * pair : 2 * hd * (pair + 1)],
                    wbuf.at[kind, pair],
                    load_sem.at[1 + 3 * pair + kind],
                )
            )
    part = hg * hd

    def wo_slices(wave, side):
        src = wo_hbm.at[wave * part : (wave + 1) * part, pl.ds(pl.multiple_of(side * cols, cols), cols)]
        return src, wobuf.at[wave, pl.ds(pl.multiple_of(half * part, part), part)]

    wo_own = [pltpu.make_async_copy(*wo_slices(wave, half), load_sem.at[1 + 3 * hg + wave]) for wave in range(2)]
    for copy in loads:
        copy.start()

    partner = (1 - half, me)
    barrier = pltpu.get_barrier_semaphore()
    for axis in range(3):
        for by in (1, -1):
            pl.semaphore_signal(barrier, inc=1, device_id=(half, neighbour(me, axis, by)), device_id_type=MESH)
    pl.semaphore_signal(barrier, inc=1, device_id=partner, device_id_type=MESH)
    pl.semaphore_wait(barrier, 7)

    x_copy = remote(x_hbm, xbuf.at[half], pair_send.at[0], pair_recv.at[0], partner)
    x_copy.start()
    wo_copy = [
        remote(*wo_slices(wave, 1 - half), pair_send.at[1 + wave], pair_recv.at[1 + wave], partner) for wave in range(2)
    ]

    ids = ids_ref[...]
    used = lax.broadcasted_iota(jnp.int32, ids.shape, 1) < cnt_ref[...]
    wanted = lax.broadcasted_iota(jnp.int32, (TABLE, 1), 0) + (me - CENTRE)
    hit = jnp.where((ids == wanted) & used, 0.0, NEG)
    table[0] = jnp.broadcast_to(jnp.max(hit, axis=1, keepdims=True), (TABLE, hd))
    tab_copies = []
    for axis in range(3):
        for e, by in enumerate((1, -1)):
            tab_copies.append(
                remote(
                    table.at[0], table.at[2 + 2 * axis - e], tab_send.at[2 * axis + e],
                    tab_recv.at[2 * axis + 1 - e], (half, neighbour(me, axis, by)),
                )
            )
    for copy in tab_copies:
        copy.start()

    def kv_dst(h, grp, e):
        return kbuf.at[h, grp, pl.ds(e * tile, tile)], vbuf.at[h, grp, :, e * tile : (e + 1) * tile]

    def own_copies(h, roles=(1, 2)):
        o = h % 3
        out = []
        for role in roles:
            grp = role
            for e, by in enumerate((1, -1)):
                device = (half, neighbour(me, (o + role) % 3, by))
                for kv in range(2):
                    out.append(
                        remote(
                            kv_dst(h, 0, 0)[kv], kv_dst(h, grp, 1 - e)[kv], own_send.at[h, 2 * grp - 2 + e, kv],
                            kv_recv.at[h, grp, 1 - e, kv], device,
                        )
                    )
        return out

    def fwd_copies(h):
        o = h % 3
        out = []
        for b in range(2):
            for e, by in enumerate((1, -1)):
                device = (half, neighbour(me, (o + 2) % 3, by))
                for kv in range(2):
                    out.append(
                        remote(
                            kv_dst(h, 1, b)[kv], kv_dst(h, 3 + b, 1 - e)[kv], fwd_send.at[h, 2 * b + e, kv],
                            kv_recv.at[h, 3 + b, 1 - e, kv], device,
                        )
                    )
        return out

    def q_copies(h):
        return [
            remote(
                qbuf.at[h, 0:tile], qbuf.at[h, (2 - e) * tile : (3 - e) * tile], q_send.at[h, e],
                q_recv.at[h, 1 - e], (half, neighbour(me, h % 3, by)),
            )
            for e, by in enumerate((1, -1))
        ]

    def o_copies(h):
        out = []
        for e, by in enumerate((1, -1)):
            device = (half, neighbour(me, h % 3, by))
            out.append(remote(osend.at[h, e], orecv.at[h, 1 - e], o_send.at[h, e, 0], o_recv.at[h, 1 - e, 0], device))
            out.append(remote(ssend.at[h, e], srecv.at[h, 1 - e], o_send.at[h, e, 1], o_recv.at[h, 1 - e, 1], device))
        return out

    def start(copies):
        for copy in copies:
            copy.start()

    loads[0].wait()

    def own_half(pair, carry):
        for kind, ref in ((2, wq_hbm), (0, wk_hbm), (1, wv_hbm)):
            pltpu.make_async_copy(
                ref.at[:, 0 : 2 * hd], wbuf.at[kind, pair], load_sem.at[1 + 3 * pair + kind]
            ).wait()
        rows = pl.ds(pl.multiple_of(half * cols, cols), cols)
        for kind in (2, 0, 1):
            partial[kind, pair] = jnp.dot(xbuf[half], wbuf[kind, pair, rows], preferred_element_type=F32)
        return carry


    def project(kind, pair):
        rows = pl.ds(pl.multiple_of((1 - half) * cols, cols), cols)
        return partial[kind, pair] + jnp.dot(xbuf[1 - half], wbuf[kind, pair, rows], preferred_element_type=F32)

    def normal(rows, gain):
        meansq = jnp.mean(rows * rows, axis=-1, keepdims=True)
        return (rows * lax.rsqrt(meansq + 1e-06) * gain).astype(BF16)

    def one_pair(pair, carry):
        proj = project(2, pair)
        for e in range(2):
            qbuf[2 * pair + e, 0:tile, :] = normal(proj[:, e * hd : (e + 1) * hd], qg_ref[...])
        proj = project(0, pair)
        for e in range(2):
            kbuf[2 * pair + e, 0, 0:tile, :] = normal(proj[:, e * hd : (e + 1) * hd], kg_ref[...])
        proj = project(1, pair)
        for e in range(2):
            vbuf[2 * pair + e, 0, :, 0:tile] = jnp.transpose(proj[:, e * hd : (e + 1) * hd]).astype(BF16)
        @pl.when(pair == 0)
        def _():
            for h in range(2):
                start(q_copies(h) + own_copies(h, (1,)))

        @pl.when(pair == 1)
        def _():
            start(q_copies(2) + own_copies(2, (1,)))

        return carry

    lax.fori_loop(0, hg - 1, own_half, 0)
    x_copy.wait_recv()
    lax.fori_loop(0, hg - 1, one_pair, 0)
    own_half(hg - 1, 0)
    one_pair(hg - 1, 0)
    start(wo_own)
    start(wo_copy)
    for copy in tab_copies:
        copy.wait_recv()

    def shifts(h, b, g):
        o = h % 3
        sa, sb, sg = stride_of(o), stride_of((o + 1) % 3), stride_of((o + 2) % 3)
        parts = []
        for which, a in ((0, 0), (1, 1), (2, -1)):
            row = CENTRE - a * sa + b * sb + g * sg
            slot = 0 if which == 0 else 2 * o + which
            parts += [table[slot, pl.ds(row, 1), :]] * (tile // hd)
        return jnp.concatenate(parts, axis=1)

    def attend(h, work, slots=(0, 1, 2)):
        wide = [slice(c, c + w) for c, w in blocks if c // tile in slots]
        lots = [(*each, wide[n : n + 2]) for each in work for n in range(0, len(wide), 2)]
        items = [(grp, len(bias) * tile, cl) for grp, bias, first, lot in lots for cl in lot]

        def scores(grp, keys, cl, t):
            rows = slice(t * tile, (t + 1) * tile)
            return lax.dot_general(kbuf[h, grp, rows, :], qbuf[h, cl, :], NT, preferred_element_type=F32)

        def weigh(parts, bias, first, cl, following):
            later = []
            ahead = following[1] // tile if following else 0
            new = jnp.full((1, parts[0].shape[1]), FLOOR, F32) if first else top[h, 0:1, cl]
            old = new
            for part, shift in zip(parts, bias):
                new = jnp.maximum(new, jnp.max(part, axis=0, keepdims=True) + shift[:, cl])
            sums = None
            weights = []
            for part, shift in zip(parts, bias):
                if len(later) < ahead:
                    later.append(scores(*following, len(later)))
                expo = jnp.exp2(part * scale - (new - shift[:, cl]) * scale)
                weights.append(expo.astype(BF16))
                fold = jnp.sum(expo, axis=0, keepdims=True)
                sums = fold if sums is None else sums + fold
            while len(later) < ahead:
                later.append(scores(*following, len(later)))
            keep = None
            if not first:
                keep = jnp.exp2((old - new) * scale)
                sums = sums + tot[h, 0:1, cl] * keep
            tot[h, 0:1, cl] = sums
            top[h, 0:1, cl] = new
            return keep, jnp.concatenate(weights, axis=0), later

        def add(grp, keys, first, lot, done):
            cl = slice(lot[0].start, lot[-1].stop)
            new = jnp.dot(
                vbuf[h, grp, :, 0:keys], jnp.concatenate([each[1] for each in done], axis=1), preferred_element_type=F32
            )
            acc[h, :, cl] = new if first else acc[h, :, cl] * jnp.concatenate([each[0] for each in done], axis=1) + new

        s = [scores(*items[0], t) for t in range(items[0][1] // tile)]
        count = 0
        last = None
        for grp, bias, first, lot in lots:
            done = []
            for cl in lot:
                count += 1
                following = items[count] if count < len(items) else None
                done.append(weigh(s, bias, first, cl, following))
                s = done[-1][2]
            if last is not None:
                add(*last)
            last = (grp, len(bias) * tile, first, lot, done)
        add(*last)

    def arrive(h, grp):
        for e in range(2):
            for kv in range(2):
                dst = kv_dst(h, grp, e)[kv]
                remote(dst, dst, own_send.at[h, 0, kv], kv_recv.at[h, grp, e, kv], partner).wait_recv()

    def own_alone(h, carry):
        attend(h, [(0, [shifts(h, 0, 0)], True)], (0,))
        return carry

    def own_others(h, carry):
        for copy in q_copies(h):
            copy.wait_recv()
        attend(h, [(0, [shifts(h, 0, 0)], True)], (1, 2))
        return carry

    def forward(h, carry):
        start(fwd_copies(h))
        return carry

    def send_queries(h, carry):
        start(q_copies(h))
        return carry

    def send_first(h, carry):
        start(own_copies(h, (1,)))
        return carry

    def send_second(h, carry):
        start(own_copies(h, (2,)))
        return carry

    def give_back(h):
        for e in range(2):
            cl = slice((1 + e) * tile, (2 + e) * tile)
            osend[h, e] = acc[h, :, cl].astype(BF16)
            ssend[h, e, 0:1, :] = top[h, 0:1, cl]
            ssend[h, e, 1:2, :] = tot[h, 0:1, cl]
        start(o_copies(h))

    def two_groups(h, late):
        first = [shifts(h, 1, late), shifts(h, 2 * late - 1, 0 - late)]
        second = [shifts(h, 0 - late, 1), shifts(h, 0 - late, -1)]
        return [(1 + 2 * late, first, False), (2 + 2 * late, second, False)]

    def one_group(t, carry):
        block, h = t // 3, t % 3
        arrive(h, 1 + block)

        @pl.when(t == 1)
        def _():
            lax.fori_loop(hg, group, send_queries, 0)

        @pl.when(t == 2)
        def _():
            lax.fori_loop(hg, group, send_first, 0)

        @pl.when(t == 4)
        def _():
            lax.fori_loop(hg, group, send_second, 0)

        attend(h, [(1 + block, [shifts(h, 1 - block, block), shifts(h, block - 1, 0 - block)], False)])
        return carry

    def step(t, carry):
        late, rest = t // 3, t % 3
        h = 3 * (1 - late) + rest
        arrive(h, 1 + 2 * late)
        arrive(h, 2 + 2 * late)

        @pl.when(t == 2)
        def _():
            lax.fori_loop(hg, group, forward, 0)

        attend(h, two_groups(h, late))

        @pl.when(late == 1)
        def _():
            give_back(h)

        return carry

    def last_others(h, carry):
        arrive(h, 3)
        arrive(h, 4)
        attend(h, two_groups(h, 1), (1, 2))
        give_back(h)
        return carry

    def last_own(h, carry):
        attend(h, two_groups(h, 1), (0,))
        return carry

    def combine(h, carry):
        for copy in o_copies(h):
            copy.wait_recv()
        tops = [top[h, 0:1, 0:tile], srecv[h, 0, 0:1, :], srecv[h, 1, 0:1, :]]
        tots = [tot[h, 0:1, 0:tile], srecv[h, 0, 1:2, :], srecv[h, 1, 1:2, :]]
        high = jnp.maximum(tops[0], jnp.maximum(tops[1], tops[2]))
        share = [jnp.exp2((each - high) * scale) for each in tops]
        total = share[0] * tots[0] + share[1] * tots[1] + share[2] * tots[2]
        summed = acc[h, :, 0:tile] * share[0]
        for e in range(2):
            summed = summed + orecv[h, e].astype(F32) * share[1 + e]
        att = jnp.transpose(summed / total).astype(BF16)
        attbuf[h // 3, half, :, pl.ds(pl.multiple_of((h % 3) * hd, hd), hd)] = att
        return carry

    width = 2 * hd
    att_copies = [
        remote(attbuf.at[wave, half], attbuf.at[wave, half], pair_send.at[3 + wave], pair_recv.at[3 + wave], partner)
        for wave in range(2)
    ]

    def project_out(wave, side, span):
        rows = pl.ds(pl.multiple_of(side * part, part), part)
        return jnp.dot(attbuf[wave, side], wobuf[wave, rows, span], preferred_element_type=F32)

    def column(c):
        return pl.ds(pl.multiple_of(c * width, width), width)

    def out_first(c, carry):
        span = column(c)
        outacc[:, span] = project_out(0, 0, span) + project_out(0, 1, span)
        return carry

    def out_second(c, carry):
        span = column(c)
        outacc[:, span] = outacc[:, span] + project_out(1, half, span)
        return carry

    def out_third(c, carry):
        span = column(c)
        out_ref[:, span] = (outacc[:, span] + project_out(1, 1 - half, span)).astype(BF16)
        return carry

    lax.fori_loop(0, group, own_alone, 0)
    lax.fori_loop(0, hg, send_second, 0)
    lax.fori_loop(0, hg, own_others, 0)
    lax.fori_loop(0, 6, one_group, 0)
    lax.fori_loop(0, hg, forward, 0)
    lax.fori_loop(hg, group, own_others, 0)
    lax.fori_loop(0, 6, step, 0)
    lax.fori_loop(hg, group, last_others, 0)
    lax.fori_loop(0, hg, combine, 0)
    att_copies[0].start()
    lax.fori_loop(hg, group, last_own, 0)
    for copy in wo_own:
        copy.wait()
    for copy in wo_copy:
        copy.wait_recv()
    att_copies[0].wait_recv()
    lax.fori_loop(0, cols // width, out_first, 0)
    lax.fori_loop(hg, group, combine, 0)
    att_copies[1].start()
    lax.fori_loop(0, cols // width, out_second, 0)
    att_copies[1].wait_recv()
    lax.fori_loop(0, cols // width, out_third, 0)

    x_copy.wait_send()
    for copy in wo_copy + att_copies + tab_copies:
        copy.wait_send()

    def drain(h, carry):
        for copy in own_copies(h) + fwd_copies(h) + q_copies(h) + o_copies(h):
            copy.wait_send()
        return carry

    lax.fori_loop(0, group, drain, 0)


def on_device(blocks, tokens, w_query, w_key, w_value, query_gain, key_gain, w_out, key_tiles, key_counts):
    tile, cols = tokens.shape
    hd = query_gain.shape[0]
    heads = w_query.shape[1]
    group = heads // hd
    hg = group // 2
    any_space = pl.BlockSpec(memory_space=pl.ANY)
    vmem = pl.BlockSpec(memory_space=pltpu.VMEM)
    dma = pltpu.SemaphoreType.DMA
    return pl.pallas_call(
        functools.partial(kernel, blocks),
        out_shape=jax.ShapeDtypeStruct((tile, cols), BF16),
        in_specs=[any_space] * 5 + [vmem] * 4,
        out_specs=vmem,
        scratch_shapes=[
            pltpu.VMEM((2, tile, cols), BF16),
            pltpu.VMEM((3, hg, 2 * cols, 2 * hd), BF16),
            pltpu.VMEM((2, heads, cols), BF16),
            pltpu.VMEM((group, 5, 2 * tile, hd), BF16),
            pltpu.VMEM((group, 5, hd, 2 * tile), BF16),
            pltpu.VMEM((group, 3 * tile, hd), BF16),
            pltpu.VMEM((group, hd, 3 * tile), F32),
            pltpu.VMEM((group, 8, 3 * tile), F32),
            pltpu.VMEM((group, 8, 3 * tile), F32),
            pltpu.VMEM((group, 2, hd, tile), BF16),
            pltpu.VMEM((group, 2, hd, tile), BF16),
            pltpu.VMEM((group, 2, 8, tile), F32),
            pltpu.VMEM((group, 2, 8, tile), F32),
            pltpu.VMEM((2, 2, tile, hg * hd), BF16),
            pltpu.VMEM((7, TABLE, hd), F32),
            pltpu.VMEM((3, hg, tile, 2 * hd), F32),
            pltpu.VMEM((tile, cols), F32),
            dma((3 + 3 * hg,)),
            dma((5,)),
            dma((5,)),
            dma((6,)),
            dma((6,)),
            dma((group, 4, 2)),
            dma((group, 4, 2)),
            dma((group, 5, 2, 2)),
            dma((group, 2)),
            dma((group, 2)),
            dma((group, 2, 2)),
            dma((group, 2, 2)),
        ],
        compiler_params=pltpu.CompilerParams(collective_id=0, has_side_effects=True, vmem_limit_bytes=66 * 2**20 - 2**21),
        name="tile_attention",
    )(
        tokens, w_query, w_key, w_value, w_out,
        query_gain.reshape(1, hd), key_gain.reshape(1, hd), key_tiles, key_counts.reshape(1, 1),
    )


BLOCKS = tuple((c * 128, 128) for c in range(9))


def solution(mesh):
    return jax.shard_map(
        functools.partial(on_device, BLOCKS),
        mesh=mesh,
        in_specs=(
            P("seq", "heads"),
            P(None, "heads"),
            P(None, "heads"),
            P(None, "heads"),
            P(),
            P(),
            P("heads", None),
            P("seq", None),
            P("seq"),
        ),
        out_specs=P("seq", "heads"),
        check_vma=False,
    )
```

```python
import functools
import math

import jax
import jax.numpy as jnp
from jax import lax
from jax.experimental import pallas as pl
from jax.experimental.pallas import tpu as pltpu
from jax.sharding import PartitionSpec as P

MESH = pl.DeviceIdType.MESH
GRID = 4
NEG = -1e30
FLOOR = -1e20
CENTRE = 21
TABLE = 48
BF16 = jnp.bfloat16
F32 = jnp.float32
NT = (((1,), (1,)), ((), ()))


def stride_of(axis):
    return 16 + (9 * axis * axis - 33 * axis) // 2


def neighbour(me, axis, by):
    stride = stride_of(axis)
    place = (me // stride) % GRID
    return me + ((place + by + GRID) % GRID - place) * stride


def kernel(
    blocks,
    x_hbm, wq_hbm, wk_hbm, wv_hbm, wo_hbm, qg_ref, kg_ref, ids_ref, cnt_ref,
    out_ref,
    xbuf, wbuf, wobuf, kbuf, vbuf, qbuf, acc, top, tot, osend, orecv, ssend, srecv, attbuf, table, partial, outacc,
    load_sem, pair_send, pair_recv, tab_send, tab_recv,
    own_send, fwd_send, kv_recv, q_send, q_recv, o_send, o_recv,
):
    me = lax.axis_index("seq")
    half = lax.axis_index("heads")
    tile = x_hbm.shape[0]
    cols = x_hbm.shape[1]
    hd = qg_ref.shape[1]
    group = wq_hbm.shape[1] // hd
    hg = group // 2
    scale = math.log2(math.e) / math.sqrt(hd)

    def remote(src, dst, send, recv, device):
        return pltpu.make_async_remote_copy(
            src_ref=src, dst_ref=dst, send_sem=send, recv_sem=recv, device_id=device, device_id_type=MESH
        )

    loads = [pltpu.make_async_copy(x_hbm, xbuf.at[half], load_sem.at[0])]
    for pair in range(hg):
        for kind, ref in enumerate((wk_hbm, wv_hbm, wq_hbm)):
            loads.append(
                pltpu.make_async_copy(
                    ref.at[:, 2 * hd * pair : 2 * hd * (pair + 1)],
                    wbuf.at[kind, pair],
                    load_sem.at[1 + 3 * pair + kind],
                )
            )
    part = hg * hd

    def wo_slices(wave, side):
        src = wo_hbm.at[wave * part : (wave + 1) * part, pl.ds(pl.multiple_of(side * cols, cols), cols)]
        return src, wobuf.at[wave, pl.ds(pl.multiple_of(half * part, part), part)]

    wo_own = [pltpu.make_async_copy(*wo_slices(wave, half), load_sem.at[1 + 3 * hg + wave]) for wave in range(2)]
    for copy in loads:
        copy.start()

    partner = (1 - half, me)
    barrier = pltpu.get_barrier_semaphore()
    for axis in range(3):
        for by in (1, -1):
            pl.semaphore_signal(barrier, inc=1, device_id=(half, neighbour(me, axis, by)), device_id_type=MESH)
    pl.semaphore_signal(barrier, inc=1, device_id=partner, device_id_type=MESH)
    pl.semaphore_wait(barrier, 7)

    x_copy = remote(x_hbm, xbuf.at[half], pair_send.at[0], pair_recv.at[0], partner)
    x_copy.start()
    wo_copy = [
        remote(*wo_slices(wave, 1 - half), pair_send.at[1 + wave], pair_recv.at[1 + wave], partner) for wave in range(2)
    ]

    ids = ids_ref[...]
    used = lax.broadcasted_iota(jnp.int32, ids.shape, 1) < cnt_ref[...]
    wanted = lax.broadcasted_iota(jnp.int32, (TABLE, 1), 0) + (me - CENTRE)
    hit = jnp.where((ids == wanted) & used, 0.0, NEG)
    table[0] = jnp.broadcast_to(jnp.max(hit, axis=1, keepdims=True), (TABLE, hd))
    tab_copies = []
    for axis in range(3):
        for e, by in enumerate((1, -1)):
            tab_copies.append(
                remote(
                    table.at[0], table.at[2 + 2 * axis - e], tab_send.at[2 * axis + e],
                    tab_recv.at[2 * axis + 1 - e], (half, neighbour(me, axis, by)),
                )
            )
    for copy in tab_copies:
        copy.start()

    def kv_dst(h, grp, e):
        return kbuf.at[h, grp, pl.ds(e * tile, tile)], vbuf.at[h, grp, :, e * tile : (e + 1) * tile]

    def own_copies(h, roles=(1, 2)):
        o = h % 3
        out = []
        for role in roles:
            grp = role
            for e, by in enumerate((1, -1)):
                device = (half, neighbour(me, (o + role) % 3, by))
                for kv in range(2):
                    out.append(
                        remote(
                            kv_dst(h, 0, 0)[kv], kv_dst(h, grp, 1 - e)[kv], own_send.at[h, 2 * grp - 2 + e, kv],
                            kv_recv.at[h, grp, 1 - e, kv], device,
                        )
                    )
        return out

    def fwd_copies(h, tiles=(0, 1)):
        o = h % 3
        out = []
        for b in tiles:
            for e, by in enumerate((1, -1)):
                device = (half, neighbour(me, (o + 2) % 3, by))
                for kv in range(2):
                    out.append(
                        remote(
                            kv_dst(h, 1, b)[kv], kv_dst(h, 3 + b, 1 - e)[kv], fwd_send.at[h, 2 * b + e, kv],
                            kv_recv.at[h, 3 + b, 1 - e, kv], device,
                        )
                    )
        return out

    def q_copies(h):
        return [
            remote(
                qbuf.at[h, 0:tile], qbuf.at[h, (2 - e) * tile : (3 - e) * tile], q_send.at[h, e],
                q_recv.at[h, 1 - e], (half, neighbour(me, h % 3, by)),
            )
            for e, by in enumerate((1, -1))
        ]

    def o_copies(h):
        out = []
        for e, by in enumerate((1, -1)):
            device = (half, neighbour(me, h % 3, by))
            out.append(remote(osend.at[h, e], orecv.at[h, 1 - e], o_send.at[h, e, 0], o_recv.at[h, 1 - e, 0], device))
            out.append(remote(ssend.at[h, e], srecv.at[h, 1 - e], o_send.at[h, e, 1], o_recv.at[h, 1 - e, 1], device))
        return out

    def start(copies):
        for copy in copies:
            copy.start()

    loads[0].wait()

    def own_half(pair, carry):
        for kind, ref in ((2, wq_hbm), (0, wk_hbm), (1, wv_hbm)):
            pltpu.make_async_copy(
                ref.at[:, 0 : 2 * hd], wbuf.at[kind, pair], load_sem.at[1 + 3 * pair + kind]
            ).wait()
        rows = pl.ds(pl.multiple_of(half * cols, cols), cols)
        for kind in (2, 0, 1):
            partial[kind, pair] = jnp.dot(xbuf[half], wbuf[kind, pair, rows], preferred_element_type=F32)
        return carry


    def project(kind, pair):
        rows = pl.ds(pl.multiple_of((1 - half) * cols, cols), cols)
        return partial[kind, pair] + jnp.dot(xbuf[1 - half], wbuf[kind, pair, rows], preferred_element_type=F32)

    def normal(rows, gain):
        meansq = jnp.mean(rows * rows, axis=-1, keepdims=True)
        return (rows * lax.rsqrt(meansq + 1e-06) * gain).astype(BF16)

    def one_pair(pair, carry):
        proj = project(2, pair)
        for e in range(2):
            qbuf[2 * pair + e, 0:tile, :] = normal(proj[:, e * hd : (e + 1) * hd], qg_ref[...])
        proj = project(0, pair)
        for e in range(2):
            kbuf[2 * pair + e, 0, 0:tile, :] = normal(proj[:, e * hd : (e + 1) * hd], kg_ref[...])
        proj = project(1, pair)
        for e in range(2):
            vbuf[2 * pair + e, 0, :, 0:tile] = jnp.transpose(proj[:, e * hd : (e + 1) * hd]).astype(BF16)
        @pl.when(pair == 0)
        def _():
            for h in range(2):
                start(q_copies(h) + own_copies(h, (1,)))

        @pl.when(pair == 1)
        def _():
            start(q_copies(2) + own_copies(2, (1,)))

        return carry

    lax.fori_loop(0, hg - 1, own_half, 0)
    x_copy.wait_recv()
    lax.fori_loop(0, hg - 1, one_pair, 0)
    own_half(hg - 1, 0)
    one_pair(hg - 1, 0)
    start(wo_own)
    start(wo_copy)
    for copy in tab_copies:
        copy.wait_recv()

    def shifts(h, b, g):
        o = h % 3
        sa, sb, sg = stride_of(o), stride_of((o + 1) % 3), stride_of((o + 2) % 3)
        parts = []
        for which, a in ((0, 0), (1, 1), (2, -1)):
            row = CENTRE - a * sa + b * sb + g * sg
            slot = 0 if which == 0 else 2 * o + which
            parts += [table[slot, pl.ds(row, 1), :]] * (tile // hd)
        return jnp.concatenate(parts, axis=1)

    def attend(h, work, slots=(0, 1, 2)):
        wide = [slice(c, c + w) for c, w in blocks if c // tile in slots]
        lots = [(*each, wide[n : n + 2]) for each in work for n in range(0, len(wide), 2)]
        items = [(grp, len(bias) * tile, cl) for grp, bias, first, lot in lots for cl in lot]

        def scores(grp, keys, cl, t):
            rows = slice(t * tile, (t + 1) * tile)
            return lax.dot_general(kbuf[h, grp, rows, :], qbuf[h, cl, :], NT, preferred_element_type=F32)

        def weigh(parts, bias, first, cl, following):
            later = []
            ahead = following[1] // tile if following else 0
            new = jnp.full((1, parts[0].shape[1]), FLOOR, F32) if first else top[h, 0:1, cl]
            old = new
            for part, shift in zip(parts, bias):
                new = jnp.maximum(new, jnp.max(part, axis=0, keepdims=True) + shift[:, cl])
            sums = None
            weights = []
            for part, shift in zip(parts, bias):
                if len(later) < ahead:
                    later.append(scores(*following, len(later)))
                expo = jnp.exp2(part * scale - (new - shift[:, cl]) * scale)
                weights.append(expo.astype(BF16))
                fold = jnp.sum(expo, axis=0, keepdims=True)
                sums = fold if sums is None else sums + fold
            while len(later) < ahead:
                later.append(scores(*following, len(later)))
            keep = None
            if not first:
                keep = jnp.exp2((old - new) * scale)
                sums = sums + tot[h, 0:1, cl] * keep
            tot[h, 0:1, cl] = sums
            top[h, 0:1, cl] = new
            return keep, jnp.concatenate(weights, axis=0), later

        def add(grp, keys, first, lot, done):
            cl = slice(lot[0].start, lot[-1].stop)
            new = jnp.dot(
                vbuf[h, grp, :, 0:keys], jnp.concatenate([each[1] for each in done], axis=1), preferred_element_type=F32
            )
            acc[h, :, cl] = new if first else acc[h, :, cl] * jnp.concatenate([each[0] for each in done], axis=1) + new

        s = [scores(*items[0], t) for t in range(items[0][1] // tile)]
        count = 0
        last = None
        for grp, bias, first, lot in lots:
            done = []
            for cl in lot:
                count += 1
                following = items[count] if count < len(items) else None
                done.append(weigh(s, bias, first, cl, following))
                s = done[-1][2]
            if last is not None:
                add(*last)
            last = (grp, len(bias) * tile, first, lot, done)
        add(*last)

    def arrive(h, grp):
        for e in range(2):
            for kv in range(2):
                dst = kv_dst(h, grp, e)[kv]
                remote(dst, dst, own_send.at[h, 0, kv], kv_recv.at[h, grp, e, kv], partner).wait_recv()

    def own_alone(h, carry):
        attend(h, [(0, [shifts(h, 0, 0)], True)], (0,))
        return carry

    def own_others(h, carry):
        for copy in q_copies(h):
            copy.wait_recv()
        attend(h, [(0, [shifts(h, 0, 0)], True)], (1, 2))
        return carry

    def forward_first(h, carry):
        start(fwd_copies(h, (0,)))
        return carry

    def forward_second(h, carry):
        start(fwd_copies(h, (1,)))
        return carry

    def send_queries(h, carry):
        start(q_copies(h))
        return carry

    def send_first(h, carry):
        start(own_copies(h, (1,)))
        return carry

    def send_second(h, carry):
        start(own_copies(h, (2,)))
        return carry

    def give_back(h):
        for e in range(2):
            cl = slice((1 + e) * tile, (2 + e) * tile)
            osend[h, e] = acc[h, :, cl].astype(BF16)
            ssend[h, e, 0:1, :] = top[h, 0:1, cl]
            ssend[h, e, 1:2, :] = tot[h, 0:1, cl]
        start(o_copies(h))

    def one_group(h, block):
        late, odd = block // 4, block % 2
        b0 = late * (1 - 2 * odd) + (1 - late) * (1 - odd)
        b1 = late * (1 - 2 * odd) - (1 - late) * (1 - odd)
        g0 = late + (1 - late) * odd
        return [(1 + odd + 2 * late, [shifts(h, b0, g0), shifts(h, b1, 0 - g0)], False)]

    first_wave, second_wave = (0, hg), (hg, group)
    sends = {
        1: (second_wave, send_queries),
        2: (second_wave, send_first),
        4: (second_wave, send_second),
        6: (first_wave, forward_first),
        8: (first_wave, forward_second),
        10: (second_wave, forward_first),
        12: (second_wave, forward_second),
    }

    def step(t, carry):
        block, rest = t // 3, t % 3
        h = 3 * ((block // 2) % 2) + rest
        arrive(h, 1 + block % 2 + 2 * (block // 4))
        for when, (wave, send) in sends.items():

            @pl.when(t == when)
            def _(wave=wave, send=send):
                lax.fori_loop(*wave, send, 0)

        @pl.when(block == 2)
        def _():
            own_others(h, 0)

        attend(h, one_group(h, block))

        @pl.when(block == 5)
        def _():
            give_back(h)

        return carry

    def last_others(h, carry):
        arrive(h, 4)
        attend(h, one_group(h, 7), (1, 2))
        give_back(h)
        return carry

    def last_own(h, carry):
        attend(h, one_group(h, 7), (0,))
        return carry

    def combine(h, carry):
        for copy in o_copies(h):
            copy.wait_recv()
        tops = [top[h, 0:1, 0:tile], srecv[h, 0, 0:1, :], srecv[h, 1, 0:1, :]]
        tots = [tot[h, 0:1, 0:tile], srecv[h, 0, 1:2, :], srecv[h, 1, 1:2, :]]
        high = jnp.maximum(tops[0], jnp.maximum(tops[1], tops[2]))
        share = [jnp.exp2((each - high) * scale) for each in tops]
        total = share[0] * tots[0] + share[1] * tots[1] + share[2] * tots[2]
        summed = acc[h, :, 0:tile] * share[0]
        for e in range(2):
            summed = summed + orecv[h, e].astype(F32) * share[1 + e]
        att = jnp.transpose(summed / total).astype(BF16)
        attbuf[h // 3, half, :, pl.ds(pl.multiple_of((h % 3) * hd, hd), hd)] = att
        return carry

    width = 2 * hd
    att_copies = [
        remote(attbuf.at[wave, half], attbuf.at[wave, half], pair_send.at[3 + wave], pair_recv.at[3 + wave], partner)
        for wave in range(2)
    ]

    def project_out(wave, side, span):
        rows = pl.ds(pl.multiple_of(side * part, part), part)
        return jnp.dot(attbuf[wave, side], wobuf[wave, rows, span], preferred_element_type=F32)

    def column(c):
        return pl.ds(pl.multiple_of(c * width, width), width)

    def out_first(c, carry):
        span = column(c)
        outacc[:, span] = project_out(0, 0, span) + project_out(0, 1, span)
        return carry

    def out_second(c, carry):
        span = column(c)
        outacc[:, span] = outacc[:, span] + project_out(1, half, span)
        return carry

    def out_third(c, carry):
        span = column(c)
        out_ref[:, span] = (outacc[:, span] + project_out(1, 1 - half, span)).astype(BF16)
        return carry

    lax.fori_loop(0, group, own_alone, 0)
    lax.fori_loop(0, hg, send_second, 0)
    lax.fori_loop(0, hg, own_others, 0)
    lax.fori_loop(0, 21, step, 0)
    lax.fori_loop(hg, group, last_others, 0)
    lax.fori_loop(0, hg, combine, 0)
    att_copies[0].start()
    lax.fori_loop(hg, group, last_own, 0)
    for copy in wo_own:
        copy.wait()
    for copy in wo_copy:
        copy.wait_recv()
    att_copies[0].wait_recv()
    lax.fori_loop(0, cols // width, out_first, 0)
    lax.fori_loop(hg, group, combine, 0)
    att_copies[1].start()
    lax.fori_loop(0, cols // width, out_second, 0)
    att_copies[1].wait_recv()
    lax.fori_loop(0, cols // width, out_third, 0)

    x_copy.wait_send()
    for copy in wo_copy + att_copies + tab_copies:
        copy.wait_send()

    def drain(h, carry):
        for copy in own_copies(h) + fwd_copies(h) + q_copies(h) + o_copies(h):
            copy.wait_send()
        return carry

    lax.fori_loop(0, group, drain, 0)


def on_device(blocks, tokens, w_query, w_key, w_value, query_gain, key_gain, w_out, key_tiles, key_counts):
    tile, cols = tokens.shape
    hd = query_gain.shape[0]
    heads = w_query.shape[1]
    group = heads // hd
    hg = group // 2
    any_space = pl.BlockSpec(memory_space=pl.ANY)
    vmem = pl.BlockSpec(memory_space=pltpu.VMEM)
    dma = pltpu.SemaphoreType.DMA
    return pl.pallas_call(
        functools.partial(kernel, blocks),
        out_shape=jax.ShapeDtypeStruct((tile, cols), BF16),
        in_specs=[any_space] * 5 + [vmem] * 4,
        out_specs=vmem,
        scratch_shapes=[
            pltpu.VMEM((2, tile, cols), BF16),
            pltpu.VMEM((3, hg, 2 * cols, 2 * hd), BF16),
            pltpu.VMEM((2, heads, cols), BF16),
            pltpu.VMEM((group, 5, 2 * tile, hd), BF16),
            pltpu.VMEM((group, 5, hd, 2 * tile), BF16),
            pltpu.VMEM((group, 3 * tile, hd), BF16),
            pltpu.VMEM((group, hd, 3 * tile), F32),
            pltpu.VMEM((group, 8, 3 * tile), F32),
            pltpu.VMEM((group, 8, 3 * tile), F32),
            pltpu.VMEM((group, 2, hd, tile), BF16),
            pltpu.VMEM((group, 2, hd, tile), BF16),
            pltpu.VMEM((group, 2, 8, tile), F32),
            pltpu.VMEM((group, 2, 8, tile), F32),
            pltpu.VMEM((2, 2, tile, hg * hd), BF16),
            pltpu.VMEM((7, TABLE, hd), F32),
            pltpu.VMEM((3, hg, tile, 2 * hd), F32),
            pltpu.VMEM((tile, cols), F32),
            dma((3 + 3 * hg,)),
            dma((5,)),
            dma((5,)),
            dma((6,)),
            dma((6,)),
            dma((group, 4, 2)),
            dma((group, 4, 2)),
            dma((group, 5, 2, 2)),
            dma((group, 2)),
            dma((group, 2)),
            dma((group, 2, 2)),
            dma((group, 2, 2)),
        ],
        compiler_params=pltpu.CompilerParams(collective_id=0, has_side_effects=True, vmem_limit_bytes=66 * 2**20 - 2**21),
        name="tile_attention",
    )(
        tokens, w_query, w_key, w_value, w_out,
        query_gain.reshape(1, hd), key_gain.reshape(1, hd), key_tiles, key_counts.reshape(1, 1),
    )


BLOCKS = tuple((c * 128, 128) for c in range(9))


def solution(mesh):
    return jax.shard_map(
        functools.partial(on_device, BLOCKS),
        mesh=mesh,
        in_specs=(
            P("seq", "heads"),
            P(None, "heads"),
            P(None, "heads"),
            P(None, "heads"),
            P(),
            P(),
            P("heads", None),
            P("seq", None),
            P("seq"),
        ),
        out_specs=P("seq", "heads"),
        check_vma=False,
    )
```

```python
import functools
import math

import jax
import jax.numpy as jnp
from jax import lax
from jax.experimental import pallas as pl
from jax.experimental.pallas import tpu as pltpu
from jax.sharding import PartitionSpec as P

MESH = pl.DeviceIdType.MESH
GRID = 4
NEG = -1e30
FLOOR = -1e20
CENTRE = 21
TABLE = 48
BF16 = jnp.bfloat16
F32 = jnp.float32
NT = (((1,), (1,)), ((), ()))


def stride_of(axis):
    return 16 + (9 * axis * axis - 33 * axis) // 2


def neighbour(me, axis, by):
    stride = stride_of(axis)
    place = (me // stride) % GRID
    return me + ((place + by + GRID) % GRID - place) * stride


def kernel(
    blocks,
    x_hbm, wq_hbm, wk_hbm, wv_hbm, wo_hbm, qg_ref, kg_ref, ids_ref, cnt_ref,
    out_ref,
    xbuf, wbuf, wobuf, kbuf, vbuf, qbuf, acc, top, tot, osend, orecv, ssend, srecv, attbuf, table, partial, outacc,
    load_sem, pair_send, pair_recv, tab_send, tab_recv,
    own_send, fwd_send, kv_recv, q_send, q_recv, o_send, o_recv,
):
    me = lax.axis_index("seq")
    half = lax.axis_index("heads")
    tile = x_hbm.shape[0]
    cols = x_hbm.shape[1]
    hd = qg_ref.shape[1]
    group = wq_hbm.shape[1] // hd
    hg = group // 2
    scale = math.log2(math.e) / math.sqrt(hd)

    def remote(src, dst, send, recv, device):
        return pltpu.make_async_remote_copy(
            src_ref=src, dst_ref=dst, send_sem=send, recv_sem=recv, device_id=device, device_id_type=MESH
        )

    x_load = pltpu.make_async_copy(x_hbm, xbuf.at[half], load_sem.at[0])

    def weight_loads(pair):
        span = pl.ds(pl.multiple_of(2 * hd * pair, 2 * hd), 2 * hd)
        return [
            pltpu.make_async_copy(ref.at[:, span], wbuf.at[kind, pair], load_sem.at[1 + 3 * pair + kind])
            for kind, ref in enumerate((wk_hbm, wv_hbm, wq_hbm))
        ]

    part = hg * hd

    def wo_slices(wave, side):
        src = wo_hbm.at[wave * part : (wave + 1) * part, pl.ds(pl.multiple_of(side * cols, cols), cols)]
        return src, wobuf.at[wave, pl.ds(pl.multiple_of(half * part, part), part)]

    wo_own = [pltpu.make_async_copy(*wo_slices(wave, half), load_sem.at[1 + 3 * hg + wave]) for wave in range(2)]
    for copy in [x_load] + weight_loads(0) + weight_loads(1):
        copy.start()

    partner = (1 - half, me)
    barrier = pltpu.get_barrier_semaphore()
    for axis in range(3):
        for by in (1, -1):
            pl.semaphore_signal(barrier, inc=1, device_id=(half, neighbour(me, axis, by)), device_id_type=MESH)
    pl.semaphore_signal(barrier, inc=1, device_id=partner, device_id_type=MESH)
    pl.semaphore_wait(barrier, 7)

    x_load.wait()
    x_copy = remote(xbuf.at[half], xbuf.at[half], pair_send.at[0], pair_recv.at[0], partner)
    x_copy.start()
    wo_copy = [
        remote(*wo_slices(wave, 1 - half), pair_send.at[1 + wave], pair_recv.at[1 + wave], partner) for wave in range(2)
    ]

    ids = ids_ref[...]
    used = lax.broadcasted_iota(jnp.int32, ids.shape, 1) < cnt_ref[...]
    wanted = lax.broadcasted_iota(jnp.int32, (TABLE, 1), 0) + (me - CENTRE)
    hit = jnp.where((ids == wanted) & used, 0.0, NEG)
    table[0] = jnp.broadcast_to(jnp.max(hit, axis=1, keepdims=True), (TABLE, hd))
    tab_copies = []
    for axis in range(3):
        for e, by in enumerate((1, -1)):
            tab_copies.append(
                remote(
                    table.at[0], table.at[2 + 2 * axis - e], tab_send.at[2 * axis + e],
                    tab_recv.at[2 * axis + 1 - e], (half, neighbour(me, axis, by)),
                )
            )
    for copy in tab_copies:
        copy.start()

    def kv_dst(h, grp, e):
        return kbuf.at[h, grp, pl.ds(e * tile, tile)], vbuf.at[h, grp, :, e * tile : (e + 1) * tile]

    def own_copies(h, roles=(1, 2)):
        o = h % 3
        out = []
        for role in roles:
            grp = role
            for e, by in enumerate((1, -1)):
                device = (half, neighbour(me, (o + role) % 3, by))
                for kv in range(2):
                    out.append(
                        remote(
                            kv_dst(h, 0, 0)[kv], kv_dst(h, grp, 1 - e)[kv], own_send.at[h, 2 * grp - 2 + e, kv],
                            kv_recv.at[h, grp, 1 - e, kv], device,
                        )
                    )
        return out

    def fwd_copies(h, tiles=(0, 1)):
        o = h % 3
        out = []
        for b in tiles:
            for e, by in enumerate((1, -1)):
                device = (half, neighbour(me, (o + 2) % 3, by))
                for kv in range(2):
                    out.append(
                        remote(
                            kv_dst(h, 1, b)[kv], kv_dst(h, 3 + b, 1 - e)[kv], fwd_send.at[h, 2 * b + e, kv],
                            kv_recv.at[h, 3 + b, 1 - e, kv], device,
                        )
                    )
        return out

    def q_copies(h):
        return [
            remote(
                qbuf.at[h, 0:tile], qbuf.at[h, (2 - e) * tile : (3 - e) * tile], q_send.at[h, e],
                q_recv.at[h, 1 - e], (half, neighbour(me, h % 3, by)),
            )
            for e, by in enumerate((1, -1))
        ]

    def o_copies(h):
        out = []
        for e, by in enumerate((1, -1)):
            device = (half, neighbour(me, h % 3, by))
            out.append(remote(osend.at[h, e], orecv.at[h, 1 - e], o_send.at[h, e, 0], o_recv.at[h, 1 - e, 0], device))
            out.append(remote(ssend.at[h, e], srecv.at[h, 1 - e], o_send.at[h, e, 1], o_recv.at[h, 1 - e, 1], device))
        return out

    def start(copies):
        for copy in copies:
            copy.start()

    def own_half(pair, carry):
        for copy in weight_loads(pair):
            copy.wait()

        @pl.when(pair < hg - 2)
        def _():
            start(weight_loads(pair + 2))

        rows = pl.ds(pl.multiple_of(half * cols, cols), cols)
        for kind in (2, 0, 1):
            partial[kind, pair] = jnp.dot(xbuf[half], wbuf[kind, pair, rows], preferred_element_type=F32)
        return carry


    def project(kind, pair):
        rows = pl.ds(pl.multiple_of((1 - half) * cols, cols), cols)
        return partial[kind, pair] + jnp.dot(xbuf[1 - half], wbuf[kind, pair, rows], preferred_element_type=F32)

    def normal(rows, gain):
        meansq = jnp.mean(rows * rows, axis=-1, keepdims=True)
        return (rows * lax.rsqrt(meansq + 1e-06) * gain).astype(BF16)

    def one_pair(pair, carry):
        proj = project(2, pair)
        for e in range(2):
            qbuf[2 * pair + e, 0:tile, :] = normal(proj[:, e * hd : (e + 1) * hd], qg_ref[...])
        proj = project(0, pair)
        for e in range(2):
            kbuf[2 * pair + e, 0, 0:tile, :] = normal(proj[:, e * hd : (e + 1) * hd], kg_ref[...])
        proj = project(1, pair)
        for e in range(2):
            vbuf[2 * pair + e, 0, :, 0:tile] = jnp.transpose(proj[:, e * hd : (e + 1) * hd]).astype(BF16)
        @pl.when(pair == 0)
        def _():
            for h in range(2):
                start(q_copies(h) + own_copies(h, (1,)))

        @pl.when(pair == 1)
        def _():
            start(q_copies(2) + own_copies(2, (1,)))

        return carry

    lax.fori_loop(0, hg - 1, own_half, 0)
    x_copy.wait_recv()
    lax.fori_loop(0, hg - 1, one_pair, 0)
    own_half(hg - 1, 0)
    one_pair(hg - 1, 0)
    start(wo_own)
    start(wo_copy)
    for copy in tab_copies:
        copy.wait_recv()

    def shifts(h, b, g):
        o = h % 3
        sa, sb, sg = stride_of(o), stride_of((o + 1) % 3), stride_of((o + 2) % 3)
        parts = []
        for which, a in ((0, 0), (1, 1), (2, -1)):
            row = CENTRE - a * sa + b * sb + g * sg
            slot = 0 if which == 0 else 2 * o + which
            parts += [table[slot, pl.ds(row, 1), :]] * (tile // hd)
        return jnp.concatenate(parts, axis=1)

    def attend(h, work, slots=(0, 1, 2)):
        wide = [slice(c, c + w) for c, w in blocks if c // tile in slots]
        lots = [(*each, wide[n : n + 2]) for each in work for n in range(0, len(wide), 2)]
        items = [(grp, len(bias) * tile, cl) for grp, bias, first, lot in lots for cl in lot]

        def scores(grp, keys, cl, t):
            rows = slice(t * tile, (t + 1) * tile)
            return lax.dot_general(kbuf[h, grp, rows, :], qbuf[h, cl, :], NT, preferred_element_type=F32)

        def weigh(parts, bias, first, cl, following):
            later = []
            ahead = following[1] // tile if following else 0
            new = jnp.full((1, parts[0].shape[1]), FLOOR, F32) if first else top[h, 0:1, cl]
            old = new
            for part, shift in zip(parts, bias):
                new = jnp.maximum(new, jnp.max(part, axis=0, keepdims=True) + shift[:, cl])
            sums = None
            weights = []
            for part, shift in zip(parts, bias):
                if len(later) < ahead:
                    later.append(scores(*following, len(later)))
                expo = jnp.exp2(part * scale - (new - shift[:, cl]) * scale)
                weights.append(expo.astype(BF16))
                fold = jnp.sum(expo, axis=0, keepdims=True)
                sums = fold if sums is None else sums + fold
            while len(later) < ahead:
                later.append(scores(*following, len(later)))
            keep = None
            if not first:
                keep = jnp.exp2((old - new) * scale)
                sums = sums + tot[h, 0:1, cl] * keep
            tot[h, 0:1, cl] = sums
            top[h, 0:1, cl] = new
            return keep, jnp.concatenate(weights, axis=0), later

        def add(grp, keys, first, lot, done):
            cl = slice(lot[0].start, lot[-1].stop)
            new = jnp.dot(
                vbuf[h, grp, :, 0:keys], jnp.concatenate([each[1] for each in done], axis=1), preferred_element_type=F32
            )
            acc[h, :, cl] = new if first else acc[h, :, cl] * jnp.concatenate([each[0] for each in done], axis=1) + new

        s = [scores(*items[0], t) for t in range(items[0][1] // tile)]
        count = 0
        last = None
        for grp, bias, first, lot in lots:
            done = []
            for cl in lot:
                count += 1
                following = items[count] if count < len(items) else None
                done.append(weigh(s, bias, first, cl, following))
                s = done[-1][2]
            if last is not None:
                add(*last)
            last = (grp, len(bias) * tile, first, lot, done)
        add(*last)

    def arrive(h, grp):
        for e in range(2):
            for kv in range(2):
                dst = kv_dst(h, grp, e)[kv]
                remote(dst, dst, own_send.at[h, 0, kv], kv_recv.at[h, grp, e, kv], partner).wait_recv()

    def own_alone(h, carry):
        attend(h, [(0, [shifts(h, 0, 0)], True)], (0,))
        return carry

    def own_others(h, carry):
        for copy in q_copies(h):
            copy.wait_recv()
        attend(h, [(0, [shifts(h, 0, 0)], True)], (1, 2))
        return carry

    def forward_first(h, carry):
        start(fwd_copies(h, (0,)))
        return carry

    def forward_second(h, carry):
        start(fwd_copies(h, (1,)))
        return carry

    def send_queries(h, carry):
        start(q_copies(h))
        return carry

    def send_first(h, carry):
        start(own_copies(h, (1,)))
        return carry

    def send_second(h, carry):
        start(own_copies(h, (2,)))
        return carry

    def give_back(h):
        for e in range(2):
            cl = slice((1 + e) * tile, (2 + e) * tile)
            osend[h, e] = acc[h, :, cl].astype(BF16)
            ssend[h, e, 0:1, :] = top[h, 0:1, cl]
            ssend[h, e, 1:2, :] = tot[h, 0:1, cl]
        start(o_copies(h))

    def one_group(h, block):
        late, odd = block // 4, block % 2
        b0 = late * (1 - 2 * odd) + (1 - late) * (1 - odd)
        b1 = late * (1 - 2 * odd) - (1 - late) * (1 - odd)
        g0 = late + (1 - late) * odd
        return [(1 + odd + 2 * late, [shifts(h, b0, g0), shifts(h, b1, 0 - g0)], False)]

    first_wave, second_wave = (0, hg), (hg, group)
    sends = {
        1: (second_wave, send_queries),
        2: (second_wave, send_first),
        4: (second_wave, send_second),
        6: (first_wave, forward_first),
        8: (first_wave, forward_second),
        10: (second_wave, forward_first),
        12: (second_wave, forward_second),
    }

    def step(t, carry):
        block, rest = t // 3, t % 3
        h = 3 * ((block // 2) % 2) + rest
        arrive(h, 1 + block % 2 + 2 * (block // 4))
        for when, (wave, send) in sends.items():

            @pl.when(t == when)
            def _(wave=wave, send=send):
                lax.fori_loop(*wave, send, 0)

        @pl.when(block == 2)
        def _():
            own_others(h, 0)

        attend(h, one_group(h, block))

        @pl.when(block == 5)
        def _():
            give_back(h)

        return carry

    def last_others(h, carry):
        arrive(h, 4)
        attend(h, one_group(h, 7), (1, 2))
        give_back(h)
        return carry

    def last_own(h, carry):
        attend(h, one_group(h, 7), (0,))
        return carry

    def combine(h, carry):
        for copy in o_copies(h):
            copy.wait_recv()
        tops = [top[h, 0:1, 0:tile], srecv[h, 0, 0:1, :], srecv[h, 1, 0:1, :]]
        tots = [tot[h, 0:1, 0:tile], srecv[h, 0, 1:2, :], srecv[h, 1, 1:2, :]]
        high = jnp.maximum(tops[0], jnp.maximum(tops[1], tops[2]))
        share = [jnp.exp2((each - high) * scale) for each in tops]
        total = share[0] * tots[0] + share[1] * tots[1] + share[2] * tots[2]
        summed = acc[h, :, 0:tile] * share[0]
        for e in range(2):
            summed = summed + orecv[h, e].astype(F32) * share[1 + e]
        att = jnp.transpose(summed / total).astype(BF16)
        attbuf[h // 3, half, :, pl.ds(pl.multiple_of((h % 3) * hd, hd), hd)] = att
        return carry

    width = 2 * hd
    att_copies = [
        remote(attbuf.at[wave, half], attbuf.at[wave, half], pair_send.at[3 + wave], pair_recv.at[3 + wave], partner)
        for wave in range(2)
    ]

    def project_out(wave, side, span):
        rows = pl.ds(pl.multiple_of(side * part, part), part)
        return jnp.dot(attbuf[wave, side], wobuf[wave, rows, span], preferred_element_type=F32)

    def column(c):
        return pl.ds(pl.multiple_of(c * width, width), width)

    def out_first(c, carry):
        span = column(c)
        outacc[:, span] = project_out(0, 0, span) + project_out(0, 1, span)
        return carry

    def out_second(c, carry):
        span = column(c)
        outacc[:, span] = outacc[:, span] + project_out(1, half, span)
        return carry

    def out_third(c, carry):
        span = column(c)
        out_ref[:, span] = (outacc[:, span] + project_out(1, 1 - half, span)).astype(BF16)
        return carry

    lax.fori_loop(0, group, own_alone, 0)
    lax.fori_loop(0, hg, send_second, 0)
    lax.fori_loop(0, hg, own_others, 0)
    lax.fori_loop(0, 21, step, 0)
    lax.fori_loop(hg, group, last_others, 0)
    lax.fori_loop(0, hg, combine, 0)
    att_copies[0].start()
    lax.fori_loop(hg, group, last_own, 0)
    for copy in wo_own:
        copy.wait()
    for copy in wo_copy:
        copy.wait_recv()
    att_copies[0].wait_recv()
    lax.fori_loop(0, cols // width, out_first, 0)
    lax.fori_loop(hg, group, combine, 0)
    att_copies[1].start()
    lax.fori_loop(0, cols // width, out_second, 0)
    att_copies[1].wait_recv()
    lax.fori_loop(0, cols // width, out_third, 0)

    x_copy.wait_send()
    for copy in wo_copy + att_copies + tab_copies:
        copy.wait_send()

    def drain(h, carry):
        for copy in own_copies(h) + fwd_copies(h) + q_copies(h) + o_copies(h):
            copy.wait_send()
        return carry

    lax.fori_loop(0, group, drain, 0)


def on_device(blocks, tokens, w_query, w_key, w_value, query_gain, key_gain, w_out, key_tiles, key_counts):
    tile, cols = tokens.shape
    hd = query_gain.shape[0]
    heads = w_query.shape[1]
    group = heads // hd
    hg = group // 2
    any_space = pl.BlockSpec(memory_space=pl.ANY)
    vmem = pl.BlockSpec(memory_space=pltpu.VMEM)
    dma = pltpu.SemaphoreType.DMA
    return pl.pallas_call(
        functools.partial(kernel, blocks),
        out_shape=jax.ShapeDtypeStruct((tile, cols), BF16),
        in_specs=[any_space] * 5 + [vmem] * 4,
        out_specs=vmem,
        scratch_shapes=[
            pltpu.VMEM((2, tile, cols), BF16),
            pltpu.VMEM((3, hg, 2 * cols, 2 * hd), BF16),
            pltpu.VMEM((2, heads, cols), BF16),
            pltpu.VMEM((group, 5, 2 * tile, hd), BF16),
            pltpu.VMEM((group, 5, hd, 2 * tile), BF16),
            pltpu.VMEM((group, 3 * tile, hd), BF16),
            pltpu.VMEM((group, hd, 3 * tile), F32),
            pltpu.VMEM((group, 8, 3 * tile), F32),
            pltpu.VMEM((group, 8, 3 * tile), F32),
            pltpu.VMEM((group, 2, hd, tile), BF16),
            pltpu.VMEM((group, 2, hd, tile), BF16),
            pltpu.VMEM((group, 2, 8, tile), F32),
            pltpu.VMEM((group, 2, 8, tile), F32),
            pltpu.VMEM((2, 2, tile, hg * hd), BF16),
            pltpu.VMEM((7, TABLE, hd), F32),
            pltpu.VMEM((3, hg, tile, 2 * hd), F32),
            pltpu.VMEM((tile, cols), F32),
            dma((3 + 3 * hg,)),
            dma((5,)),
            dma((5,)),
            dma((6,)),
            dma((6,)),
            dma((group, 4, 2)),
            dma((group, 4, 2)),
            dma((group, 5, 2, 2)),
            dma((group, 2)),
            dma((group, 2)),
            dma((group, 2, 2)),
            dma((group, 2, 2)),
        ],
        compiler_params=pltpu.CompilerParams(collective_id=0, has_side_effects=True, vmem_limit_bytes=66 * 2**20 - 2**21),
        name="tile_attention",
    )(
        tokens, w_query, w_key, w_value, w_out,
        query_gain.reshape(1, hd), key_gain.reshape(1, hd), key_tiles, key_counts.reshape(1, 1),
    )


BLOCKS = tuple((c * 128, 128) for c in range(9))


def solution(mesh):
    return jax.shard_map(
        functools.partial(on_device, BLOCKS),
        mesh=mesh,
        in_specs=(
            P("seq", "heads"),
            P(None, "heads"),
            P(None, "heads"),
            P(None, "heads"),
            P(),
            P(),
            P("heads", None),
            P("seq", None),
            P("seq"),
        ),
        out_specs=P("seq", "heads"),
        check_vma=False,
    )
```

```python
import functools
import math

import jax
import jax.numpy as jnp
from jax import lax
from jax.experimental import pallas as pl
from jax.experimental.pallas import tpu as pltpu
from jax.sharding import PartitionSpec as P

MESH = pl.DeviceIdType.MESH
GRID = 4
NEG = -1e30
FLOOR = -1e20
CENTRE = 21
TABLE = 48
BF16 = jnp.bfloat16
F32 = jnp.float32
NT = (((1,), (1,)), ((), ()))


def stride_of(axis):
    return 16 + (9 * axis * axis - 33 * axis) // 2


def neighbour(me, axis, by):
    stride = stride_of(axis)
    place = (me // stride) % GRID
    return me + ((place + by + GRID) % GRID - place) * stride


def kernel(
    blocks,
    x_hbm, wq_hbm, wk_hbm, wv_hbm, wo_hbm, qg_ref, kg_ref, ids_ref, cnt_ref,
    out_ref,
    xbuf, wbuf, wobuf, kbuf, vbuf, qbuf, acc, top, tot, osend, orecv, ssend, srecv, attbuf, table, partial, outacc,
    load_sem, pair_send, pair_recv, tab_send, tab_recv,
    own_send, fwd_send, kv_recv, q_send, q_recv, o_send, o_recv,
):
    me = lax.axis_index("seq")
    half = lax.axis_index("heads")
    tile = x_hbm.shape[0]
    cols = x_hbm.shape[1]
    hd = qg_ref.shape[1]
    group = wq_hbm.shape[1] // hd
    hg = group // 2
    scale = math.log2(math.e) / math.sqrt(hd)

    def remote(src, dst, send, recv, device):
        return pltpu.make_async_remote_copy(
            src_ref=src, dst_ref=dst, send_sem=send, recv_sem=recv, device_id=device, device_id_type=MESH
        )

    x_load = pltpu.make_async_copy(x_hbm, xbuf.at[half], load_sem.at[0])

    def weight_loads(pair):
        span = pl.ds(pl.multiple_of(2 * hd * pair, 2 * hd), 2 * hd)
        return [
            pltpu.make_async_copy(ref.at[:, span], wbuf.at[kind, pair], load_sem.at[1 + 3 * pair + kind])
            for kind, ref in enumerate((wk_hbm, wv_hbm, wq_hbm))
        ]

    part = hg * hd

    def wo_slices(wave, side):
        src = wo_hbm.at[wave * part : (wave + 1) * part, pl.ds(pl.multiple_of(side * cols, cols), cols)]
        return src, wobuf.at[wave, pl.ds(pl.multiple_of(half * part, part), part)]

    wo_own = [pltpu.make_async_copy(*wo_slices(wave, half), load_sem.at[1 + 3 * hg + wave]) for wave in range(2)]
    for copy in [x_load] + weight_loads(0) + weight_loads(1):
        copy.start()

    partner = (1 - half, me)
    barrier = pltpu.get_barrier_semaphore()
    for axis in range(3):
        for by in (1, -1):
            pl.semaphore_signal(barrier, inc=1, device_id=(half, neighbour(me, axis, by)), device_id_type=MESH)
    pl.semaphore_signal(barrier, inc=1, device_id=partner, device_id_type=MESH)
    pl.semaphore_wait(barrier, 7)

    x_load.wait()
    x_copy = remote(xbuf.at[half], xbuf.at[half], pair_send.at[0], pair_recv.at[0], partner)
    x_copy.start()
    wo_copy = [
        remote(*wo_slices(wave, 1 - half), pair_send.at[1 + wave], pair_recv.at[1 + wave], partner) for wave in range(2)
    ]

    ids = ids_ref[...]
    used = lax.broadcasted_iota(jnp.int32, ids.shape, 1) < cnt_ref[...]
    wanted = lax.broadcasted_iota(jnp.int32, (TABLE, 1), 0) + (me - CENTRE)
    hit = jnp.where((ids == wanted) & used, 0.0, NEG)
    table[0] = jnp.broadcast_to(jnp.max(hit, axis=1, keepdims=True), (TABLE, hd))
    tab_copies = []
    for axis in range(3):
        for e, by in enumerate((1, -1)):
            tab_copies.append(
                remote(
                    table.at[0], table.at[2 + 2 * axis - e], tab_send.at[2 * axis + e],
                    tab_recv.at[2 * axis + 1 - e], (half, neighbour(me, axis, by)),
                )
            )
    for copy in tab_copies:
        copy.start()

    def kv_dst(h, grp, e):
        return kbuf.at[h, grp, pl.ds(e * tile, tile)], vbuf.at[h, grp, :, e * tile : (e + 1) * tile]

    def own_copies(h, roles=(1, 2)):
        o = h % 3
        out = []
        for role in roles:
            grp = role
            for e, by in enumerate((1, -1)):
                device = (half, neighbour(me, (o + role) % 3, by))
                for kv in range(2):
                    out.append(
                        remote(
                            kv_dst(h, 0, 0)[kv], kv_dst(h, grp, 1 - e)[kv], own_send.at[h, 2 * grp - 2 + e, kv],
                            kv_recv.at[h, grp, 1 - e, kv], device,
                        )
                    )
        return out

    def fwd_copies(h, tiles=(0, 1)):
        o = h % 3
        out = []
        for b in tiles:
            for e, by in enumerate((1, -1)):
                device = (half, neighbour(me, (o + 2) % 3, by))
                for kv in range(2):
                    out.append(
                        remote(
                            kv_dst(h, 1, b)[kv], kv_dst(h, 3 + b, 1 - e)[kv], fwd_send.at[h, 2 * b + e, kv],
                            kv_recv.at[h, 3 + b, 1 - e, kv], device,
                        )
                    )
        return out

    def q_copies(h):
        return [
            remote(
                qbuf.at[h, 0:tile], qbuf.at[h, (2 - e) * tile : (3 - e) * tile], q_send.at[h, e],
                q_recv.at[h, 1 - e], (half, neighbour(me, h % 3, by)),
            )
            for e, by in enumerate((1, -1))
        ]

    def o_copies(h):
        out = []
        for e, by in enumerate((1, -1)):
            device = (half, neighbour(me, h % 3, by))
            out.append(remote(osend.at[h, e], orecv.at[h, 1 - e], o_send.at[h, e, 0], o_recv.at[h, 1 - e, 0], device))
            out.append(remote(ssend.at[h, e], srecv.at[h, 1 - e], o_send.at[h, e, 1], o_recv.at[h, 1 - e, 1], device))
        return out

    def start(copies):
        for copy in copies:
            copy.start()

    def own_half(pair, carry):
        for copy in weight_loads(pair):
            copy.wait()

        @pl.when(pair < hg - 2)
        def _():
            start(weight_loads(pair + 2))

        rows = pl.ds(pl.multiple_of(half * cols, cols), cols)
        for kind in (2, 0, 1):
            partial[kind, pair] = jnp.dot(xbuf[half], wbuf[kind, pair, rows], preferred_element_type=F32)
        return carry


    def project(kind, pair):
        rows = pl.ds(pl.multiple_of((1 - half) * cols, cols), cols)
        return partial[kind, pair] + jnp.dot(xbuf[1 - half], wbuf[kind, pair, rows], preferred_element_type=F32)

    def normal(rows, gain):
        meansq = jnp.mean(rows * rows, axis=-1, keepdims=True)
        return (rows * lax.rsqrt(meansq + 1e-06) * gain).astype(BF16)

    def one_pair(pair, carry):
        proj = project(2, pair)
        for e in range(2):
            qbuf[2 * pair + e, 0:tile, :] = normal(proj[:, e * hd : (e + 1) * hd], qg_ref[...])
        proj = project(0, pair)
        for e in range(2):
            kbuf[2 * pair + e, 0, 0:tile, :] = normal(proj[:, e * hd : (e + 1) * hd], kg_ref[...])
        proj = project(1, pair)
        for e in range(2):
            vbuf[2 * pair + e, 0, :, 0:tile] = jnp.transpose(proj[:, e * hd : (e + 1) * hd]).astype(BF16)
        @pl.when(pair == 0)
        def _():
            for h in range(2):
                start(q_copies(h) + own_copies(h, (1,)))

        @pl.when(pair == 1)
        def _():
            start(q_copies(2) + own_copies(2, (1,)))

        return carry

    lax.fori_loop(0, hg - 1, own_half, 0)
    x_copy.wait_recv()
    lax.fori_loop(0, hg - 1, one_pair, 0)
    own_half(hg - 1, 0)
    one_pair(hg - 1, 0)
    start(wo_own)
    start(wo_copy)
    for copy in tab_copies:
        copy.wait_recv()

    def shifts(h, b, g):
        o = h % 3
        sa, sb, sg = stride_of(o), stride_of((o + 1) % 3), stride_of((o + 2) % 3)
        parts = []
        for which, a in ((0, 0), (1, 1), (2, -1)):
            row = CENTRE - a * sa + b * sb + g * sg
            slot = 0 if which == 0 else 2 * o + which
            parts += [table[slot, pl.ds(row, 1), :]] * (tile // hd)
        return jnp.concatenate(parts, axis=1)

    def attend(h, work, slots=(0, 1, 2)):
        wide = [slice(c, c + w) for c, w in blocks if c // tile in slots]
        lots = [(*each, wide[n : n + 2]) for each in work for n in range(0, len(wide), 2)]
        items = [(grp, len(bias) * tile, cl) for grp, bias, first, lot in lots for cl in lot]

        def scores(grp, keys, cl, t):
            rows = slice(t * tile, (t + 1) * tile)
            return lax.dot_general(kbuf[h, grp, rows, :], qbuf[h, cl, :], NT, preferred_element_type=F32)

        def weigh(parts, bias, first, cl, following):
            later = []
            ahead = following[1] // tile if following else 0
            new = jnp.full((1, parts[0].shape[1]), FLOOR, F32) if first else top[h, 0:1, cl]
            old = new
            for part, shift in zip(parts, bias):
                new = jnp.maximum(new, jnp.max(part, axis=0, keepdims=True) + shift[:, cl])
            sums = None
            weights = []
            for part, shift in zip(parts, bias):
                if len(later) < ahead:
                    later.append(scores(*following, len(later)))
                expo = jnp.exp2(part * scale - (new - shift[:, cl]) * scale)
                weights.append(expo.astype(BF16))
                fold = jnp.sum(expo, axis=0, keepdims=True)
                sums = fold if sums is None else sums + fold
            while len(later) < ahead:
                later.append(scores(*following, len(later)))
            keep = None
            if not first:
                keep = jnp.exp2((old - new) * scale)
                sums = sums + tot[h, 0:1, cl] * keep
            tot[h, 0:1, cl] = sums
            top[h, 0:1, cl] = new
            return keep, jnp.concatenate(weights, axis=0), later

        def add(grp, keys, first, lot, done):
            cl = slice(lot[0].start, lot[-1].stop)
            new = jnp.dot(
                vbuf[h, grp, :, 0:keys], jnp.concatenate([each[1] for each in done], axis=1), preferred_element_type=F32
            )
            acc[h, :, cl] = new if first else acc[h, :, cl] * jnp.concatenate([each[0] for each in done], axis=1) + new

        s = [scores(*items[0], t) for t in range(items[0][1] // tile)]
        count = 0
        last = None
        for grp, bias, first, lot in lots:
            done = []
            for cl in lot:
                count += 1
                following = items[count] if count < len(items) else None
                done.append(weigh(s, bias, first, cl, following))
                s = done[-1][2]
            if last is not None:
                add(*last)
            last = (grp, len(bias) * tile, first, lot, done)
        add(*last)

    def arrive(h, grp):
        for e in range(2):
            for kv in range(2):
                dst = kv_dst(h, grp, e)[kv]
                remote(dst, dst, own_send.at[h, 0, kv], kv_recv.at[h, grp, e, kv], partner).wait_recv()

    def own_alone(h, carry):
        attend(h, [(0, [shifts(h, 0, 0)], True)], (0,))
        return carry

    def own_others(h, carry):
        for copy in q_copies(h):
            copy.wait_recv()
        attend(h, [(0, [shifts(h, 0, 0)], True)], (1, 2))
        return carry

    def forward_first(h, carry):
        start(fwd_copies(h, (0,)))
        return carry

    def forward_second(h, carry):
        start(fwd_copies(h, (1,)))
        return carry

    def send_queries(h, carry):
        start(q_copies(h))
        return carry

    def send_first(h, carry):
        start(own_copies(h, (1,)))
        return carry

    def send_second(h, carry):
        start(own_copies(h, (2,)))
        return carry

    def give_back(h):
        for e in range(2):
            cl = slice((1 + e) * tile, (2 + e) * tile)
            osend[h, e] = acc[h, :, cl].astype(BF16)
            ssend[h, e, 0:1, :] = top[h, 0:1, cl]
            ssend[h, e, 1:2, :] = tot[h, 0:1, cl]
        start(o_copies(h))

    def one_group(h, block):
        late, odd = block // 4, block % 2
        b0 = late * (1 - 2 * odd) + (1 - late) * (1 - odd)
        b1 = late * (1 - 2 * odd) - (1 - late) * (1 - odd)
        g0 = late + (1 - late) * odd
        return [(1 + odd + 2 * late, [shifts(h, b0, g0), shifts(h, b1, 0 - g0)], False)]

    first_wave, second_wave = (0, hg), (hg, group)
    sends = {
        0: (second_wave, send_queries),
        1: (second_wave, send_first),
        3: (second_wave, send_second),
        5: (first_wave, forward_first),
        6: (first_wave, forward_second),
        9: (second_wave, forward_first),
        11: (second_wave, forward_second),
    }

    def step(t, carry):
        block, rest = t // 3, t % 3
        h = 3 * ((block // 2) % 2) + rest
        arrive(h, 1 + block % 2 + 2 * (block // 4))
        for when, (wave, send) in sends.items():

            @pl.when(t == when)
            def _(wave=wave, send=send):
                lax.fori_loop(*wave, send, 0)

        @pl.when(block == 2)
        def _():
            own_others(h, 0)

        attend(h, one_group(h, block))

        @pl.when(block == 5)
        def _():
            give_back(h)

        return carry

    def last_others(h, carry):
        arrive(h, 4)
        attend(h, one_group(h, 7), (1, 2))
        give_back(h)
        return carry

    def last_own(h, carry):
        attend(h, one_group(h, 7), (0,))
        return carry

    def combine(h, carry):
        for copy in o_copies(h):
            copy.wait_recv()
        tops = [top[h, 0:1, 0:tile], srecv[h, 0, 0:1, :], srecv[h, 1, 0:1, :]]
        tots = [tot[h, 0:1, 0:tile], srecv[h, 0, 1:2, :], srecv[h, 1, 1:2, :]]
        high = jnp.maximum(tops[0], jnp.maximum(tops[1], tops[2]))
        share = [jnp.exp2((each - high) * scale) for each in tops]
        total = share[0] * tots[0] + share[1] * tots[1] + share[2] * tots[2]
        summed = acc[h, :, 0:tile] * share[0]
        for e in range(2):
            summed = summed + orecv[h, e].astype(F32) * share[1 + e]
        att = jnp.transpose(summed / total).astype(BF16)
        attbuf[h // 3, half, :, pl.ds(pl.multiple_of((h % 3) * hd, hd), hd)] = att
        return carry

    width = 2 * hd
    att_copies = [
        remote(attbuf.at[wave, half], attbuf.at[wave, half], pair_send.at[3 + wave], pair_recv.at[3 + wave], partner)
        for wave in range(2)
    ]

    def project_out(wave, side, span):
        rows = pl.ds(pl.multiple_of(side * part, part), part)
        return jnp.dot(attbuf[wave, side], wobuf[wave, rows, span], preferred_element_type=F32)

    def column(c):
        return pl.ds(pl.multiple_of(c * width, width), width)

    def out_first(c, carry):
        span = column(c)
        outacc[:, span] = project_out(0, 0, span) + project_out(0, 1, span)
        return carry

    def out_second(c, carry):
        span = column(c)
        outacc[:, span] = outacc[:, span] + project_out(1, half, span)
        return carry

    def out_third(c, carry):
        span = column(c)
        out_ref[:, span] = (outacc[:, span] + project_out(1, 1 - half, span)).astype(BF16)
        return carry

    lax.fori_loop(0, group, own_alone, 0)
    lax.fori_loop(0, hg, send_second, 0)
    lax.fori_loop(0, hg, own_others, 0)
    lax.fori_loop(0, 21, step, 0)
    lax.fori_loop(hg, group, last_others, 0)
    lax.fori_loop(0, hg, combine, 0)
    att_copies[0].start()
    lax.fori_loop(hg, group, last_own, 0)
    for copy in wo_own:
        copy.wait()
    for copy in wo_copy:
        copy.wait_recv()
    att_copies[0].wait_recv()
    lax.fori_loop(0, cols // width, out_first, 0)
    lax.fori_loop(hg, group, combine, 0)
    att_copies[1].start()
    lax.fori_loop(0, cols // width, out_second, 0)
    att_copies[1].wait_recv()
    lax.fori_loop(0, cols // width, out_third, 0)

    x_copy.wait_send()
    for copy in wo_copy + att_copies + tab_copies:
        copy.wait_send()

    def drain(h, carry):
        for copy in own_copies(h) + fwd_copies(h) + q_copies(h) + o_copies(h):
            copy.wait_send()
        return carry

    lax.fori_loop(0, group, drain, 0)


def on_device(blocks, tokens, w_query, w_key, w_value, query_gain, key_gain, w_out, key_tiles, key_counts):
    tile, cols = tokens.shape
    hd = query_gain.shape[0]
    heads = w_query.shape[1]
    group = heads // hd
    hg = group // 2
    any_space = pl.BlockSpec(memory_space=pl.ANY)
    vmem = pl.BlockSpec(memory_space=pltpu.VMEM)
    dma = pltpu.SemaphoreType.DMA
    return pl.pallas_call(
        functools.partial(kernel, blocks),
        out_shape=jax.ShapeDtypeStruct((tile, cols), BF16),
        in_specs=[any_space] * 5 + [vmem] * 4,
        out_specs=vmem,
        scratch_shapes=[
            pltpu.VMEM((2, tile, cols), BF16),
            pltpu.VMEM((3, hg, 2 * cols, 2 * hd), BF16),
            pltpu.VMEM((2, heads, cols), BF16),
            pltpu.VMEM((group, 5, 2 * tile, hd), BF16),
            pltpu.VMEM((group, 5, hd, 2 * tile), BF16),
            pltpu.VMEM((group, 3 * tile, hd), BF16),
            pltpu.VMEM((group, hd, 3 * tile), F32),
            pltpu.VMEM((group, 8, 3 * tile), F32),
            pltpu.VMEM((group, 8, 3 * tile), F32),
            pltpu.VMEM((group, 2, hd, tile), BF16),
            pltpu.VMEM((group, 2, hd, tile), BF16),
            pltpu.VMEM((group, 2, 8, tile), F32),
            pltpu.VMEM((group, 2, 8, tile), F32),
            pltpu.VMEM((2, 2, tile, hg * hd), BF16),
            pltpu.VMEM((7, TABLE, hd), F32),
            pltpu.VMEM((3, hg, tile, 2 * hd), F32),
            pltpu.VMEM((tile, cols), F32),
            dma((3 + 3 * hg,)),
            dma((5,)),
            dma((5,)),
            dma((6,)),
            dma((6,)),
            dma((group, 4, 2)),
            dma((group, 4, 2)),
            dma((group, 5, 2, 2)),
            dma((group, 2)),
            dma((group, 2)),
            dma((group, 2, 2)),
            dma((group, 2, 2)),
        ],
        compiler_params=pltpu.CompilerParams(collective_id=0, has_side_effects=True, vmem_limit_bytes=66 * 2**20 - 2**21),
        name="tile_attention",
    )(
        tokens, w_query, w_key, w_value, w_out,
        query_gain.reshape(1, hd), key_gain.reshape(1, hd), key_tiles, key_counts.reshape(1, 1),
    )


BLOCKS = tuple((c * 128, 128) for c in range(9))


def solution(mesh):
    return jax.shard_map(
        functools.partial(on_device, BLOCKS),
        mesh=mesh,
        in_specs=(
            P("seq", "heads"),
            P(None, "heads"),
            P(None, "heads"),
            P(None, "heads"),
            P(),
            P(),
            P("heads", None),
            P("seq", None),
            P("seq"),
        ),
        out_specs=P("seq", "heads"),
        check_vma=False,
    )
```
